32 devices in a mesh: group: 2 (over x), trade: 16 (over z, y, core).
Axes of the slice: x: 2, y: 2, z: 4, core: 2. Of those that a mesh axis runs over, the one named last changes fastest.
Arguments:
- factors: bfloat16 [128, 128], P(('group', 'trade')), parts along dimension 0, may hold values from -6 to 6
- loadings: float32 [32, 16], replicated, may hold values from -1.5 to 1.5
- trade_coef: bfloat16 [65536, 256], P(('group', 'trade')), parts along dimension 0, may hold values from -0.75 to 0.75
- basis_size: int32 [65536], P(('group', 'trade')), parts along dimension 0, may hold values from 4 to 32
- set_ids: int32 [65536], P(('group', 'trade')), parts along dimension 0, may hold values from 0 to 31
- live_count: int32 [32], P(('group', 'trade')), parts along dimension 0, may hold values from 1 to 2047, as said below
- netting_row: int32 [64], P('group'), parts along dimension 0, may hold values from 0 to 31, each once
- threshold: float32 [64], P(('group', 'trade')), parts along dimension 0, may hold values from 0.5 to 8
- margin_start: float32 [64, 64], P(('group', 'trade')), parts along dimension 0, may hold values from 0 to 3
Outputs:
- expected: float32 [64, 8], P(('group', 'trade')), parts along dimension 0
The draws below stay inside these ranges and needn't reach their ends.
There are 2 independent parts, one for each index of `group`. The reference program is written for one: setup_inputs(seed, part) draws one part's arguments, and reference() takes and returns one part's arrays. A program takes and returns all parts, laid end to end along the dimension named above; an argument that names none is the same for every part. Nothing has to cross between parts.
Inputs may be any that keep to these rules, and one draw needn't show every extreme that they name: `live_count`: blocks b and b + 8 hold exactly 2048 live trades together.
All inputs are finite; a program needn't handle non-finite values.
Results may differ from the reference program's by a relative error of at most 0.00035.
Values may be sent and summed in bfloat16 or wider, within the bound.
A program may use at most 64 MiB of HBM per device.

```python
import math
import jax
import jax.numpy as jnp
import numpy as np
from jax import lax

F = 16
K = 32
DATES = 8
LAG = 2
AVG = 1024
SLOTS = 2048
BLOCKS = 16
TRADES = 32768
P_SIZE = 64
NS = 32


def draw_live_count(key, part):
    half_blocks = BLOCKS // 2
    first_key, second_key = jax.random.split(jax.random.fold_in(key, 11))
    lower = jax.random.randint(first_key, (half_blocks,), 1, 2 * AVG, dtype=jnp.int32)
    heavy = jax.random.randint(second_key, (), 0, half_blocks, dtype=jnp.int32)
    lower = jnp.where(jnp.arange(half_blocks, dtype=jnp.int32) == heavy, 2 * AVG - 1, lower)
    return jnp.concatenate([lower, 2 * AVG - lower]).astype(jnp.int32)


def set_ends(result, rng, smallest, top_value):
    spot = [jax.random.randint(jax.random.fold_in(rng, axis), (), 0, length) for axis, length in enumerate(result.shape)]
    widest = result.shape.index(max(result.shape))
    neighbour = spot[:widest] + [(spot[widest] + 1) % result.shape[widest]] + spot[widest + 1:]
    return result.at[tuple(spot)].set(smallest).at[tuple(neighbour)].set(top_value)


def block_levels(own_key, shape, shards, smallest, top_value):
    level = 1.0
    for axis_at, parts in shards:
        draws = jax.random.uniform(jax.random.fold_in(jax.random.fold_in(own_key, 6), axis_at), (parts,), jnp.float32, smallest / len(shards), top_value / len(shards))
        level = level * jnp.repeat(jnp.exp(draws), shape[axis_at] // parts).reshape((-1,) + (1,) * (len(shape) - 1 - axis_at))
    return level


def rank_table(count, slope):
    portions = [(1 << 20) // math.isqrt(standing ** slope) + 1 for standing in range(1, count + 1)]
    spread = 1 + sum(portions) // (1 << 30)
    return np.cumsum(np.array([max(1, weight // spread) for weight in portions]))


def ranked_ids(stream_key, extent, number_of, lean):
    listing = rank_table(number_of, lean)
    lot = jax.random.randint(jax.random.fold_in(stream_key, 1), extent, 0, int(listing[number_of - 1]))
    grade = jnp.searchsorted(jnp.asarray(listing, jnp.int32), lot, side="right")
    return jax.random.permutation(jax.random.fold_in(stream_key, 2), number_of)[grade].astype(jnp.int32)


def scatter_about(key, dims, width, most, shards=(), kind=jnp.bfloat16):
    level = block_levels(key, dims, shards, -0.22, 0.18) if shards else 1.0
    entries = jax.random.normal(key, dims, jnp.float32) * width * level
    return jnp.minimum(jnp.maximum(entries, -most), most).astype(kind)


def setup_inputs(seed: int = 0, part: int = 0) -> dict:
    splits = jax.random.split(jax.random.key(seed), 10)
    own_keys = jax.random.split(jax.random.fold_in(splits[9], part), 10)
    factors = scatter_about(own_keys[0], (P_SIZE, DATES * F), 1.0, 6.0, ((0, 16),))
    loadings = scatter_about(splits[1], (K, F), F ** -0.5, 1.5, (), jnp.float32)
    trade_coef = scatter_about(own_keys[2], (TRADES, DATES * K), 0.05, 0.75, ((0, 16),))
    basis_size = set_ends(jax.random.randint(own_keys[3], (TRADES,), 4, K + 1), jax.random.fold_in(own_keys[3], 1), 4, K).astype(jnp.int32)
    set_ids = set_ends(ranked_ids(own_keys[4], (TRADES,), NS, 1), jax.random.fold_in(own_keys[4], 3), 0, NS - 1).astype(jnp.int32)
    live_count = draw_live_count(jax.random.fold_in(jax.random.fold_in(splits[9], part), 71), part)
    netting_row = jax.random.permutation(own_keys[6], NS).astype(jnp.int32)
    threshold = jnp.clip(jnp.exp(math.log(8.0) - 2.7725887 * jax.random.uniform(own_keys[7], (NS,), jnp.float32) ** block_levels(own_keys[7], (NS,), ((0, 16),), -0.2, 0.2)), 0.5, 8.0)
    margin_start = jnp.clip(3.0 * jax.random.uniform(own_keys[8], (NS, P_SIZE), jnp.float32) ** block_levels(own_keys[8], (NS, P_SIZE), ((0, 16),), -0.2, 0.2), 0.0, 3.0)
    return {"factors": factors, "loadings": loadings, "trade_coef": trade_coef, "basis_size": basis_size, "set_ids": set_ids, "live_count": live_count, "netting_row": netting_row, "threshold": threshold, "margin_start": margin_start}


def reference(factors, loadings, trade_coef, basis_size, set_ids, live_count, netting_row, threshold, margin_start):
    path_total = factors.shape[0]
    set_total = netting_row.shape[0]
    factor_cube = factors.astype(jnp.float32).reshape(path_total, DATES, F)
    basis_table = jnp.einsum("pdf,kf->pdk", factor_cube, loadings, precision=lax.Precision.HIGHEST)
    basis_table = jnp.tanh(basis_table).astype(jnp.bfloat16)
    basis_wide = basis_table.astype(jnp.float32)
    trade_rows = netting_row[set_ids].astype(jnp.int32)
    basis_index = jnp.arange(K, dtype=jnp.int32)
    slot_index = jnp.arange(SLOTS, dtype=jnp.int32)

    def add_block(block_index, running):
        first_row = (block_index * SLOTS).astype(jnp.int32)
        coef_block = lax.dynamic_slice_in_dim(trade_coef, first_row, SLOTS, 0).reshape(SLOTS, DATES, K)
        sizes_block = lax.dynamic_slice_in_dim(basis_size, first_row, SLOTS, 0)
        rows_block = lax.dynamic_slice_in_dim(trade_rows, first_row, SLOTS, 0)
        live_now = live_count[block_index]
        keep_mask = (basis_index[None, :] < sizes_block[:, None]) & (slot_index < live_now)[:, None]
        coef_used = jnp.where(keep_mask[:, None, :], coef_block, jnp.zeros_like(coef_block)).astype(jnp.bfloat16)
        values = jnp.einsum("tdk,pdk->tdp", coef_used.astype(jnp.float32), basis_wide)
        values = values.astype(jnp.bfloat16).astype(jnp.float32).reshape(SLOTS, DATES * path_total)
        return running + jax.ops.segment_sum(values, rows_block, num_segments=set_total)

    running = jnp.zeros((set_total, DATES * path_total), jnp.float32)
    running = lax.fori_loop(0, BLOCKS, add_block, running)
    netted = running.reshape(set_total, DATES, path_total)
    margin = jnp.maximum(netted[:, : DATES - LAG] - threshold[:, None, None], 0.0)
    held = jnp.broadcast_to(margin_start[:, None, :], (set_total, LAG, path_total))
    collateral = jnp.concatenate([held, margin], axis=1)
    shortfall = jnp.maximum(netted - collateral, 0.0)
    return jnp.sum(shortfall, axis=2) / path_total
```

```python
import functools

import jax
import jax.numpy as jnp
from jax import lax
from jax.experimental import pallas as pl
from jax.experimental.pallas import tpu as pltpu
from jax.sharding import PartitionSpec as P

F = 16
K = 32
DATES = 8
LAG = 2
LANES = 128
CHUNK = 256
COLS = 512
MESH = pl.DeviceIdType.MESH
f32 = jnp.float32
bf16 = jnp.bfloat16


def iota(shape, axis):
    return lax.broadcasted_iota(jnp.int32, shape, axis)


def kernel(
    n,
    factors,
    loadings,
    trade_coef,
    basis_size,
    set_ids,
    live_count,
    netting_row,
    threshold,
    margin_start,
    out,
    fact,
    load_v,
    coef_v,
    size_v,
    ids_v,
    nrow_v,
    thr_s,
    marg_v,
    split,
    onehot,
    spread,
    basis,
    held,
    acc,
    part,
    recv,
    in_sem,
    gs_sem,
    gr_sem,
    ss_sem,
    sr_sem,
):
    me = lax.axis_index("trade")
    rows = fact.shape[1]
    near = n // 2
    paths = near * rows
    rep = max(1, LANES // paths)
    width = rep * paths
    slots = coef_v.shape[0]
    owned = recv.shape[2]
    mine = lax.div(me, near)
    sets = n * owned

    quarter = n // 4
    hub = quarter + 1
    is_hub = me == hub
    is_late = me >= near
    is_first = me < quarter
    is_second = jnp.logical_and(jnp.logical_and(me >= quarter, me < near), me != hub)

    def each(step, lo, hi, among=True):
        def at(i):
            step(jnp.where(i >= me, i + 1, i) if among else i)

        count = hi - lo - 1 if among else hi - lo
        if n <= LANES // 4:
            for i in range(lo, lo + count):
                at(i)
        else:
            lax.fori_loop(lo, lo + count, lambda i, c: (at(i), c)[1], 0)

    def local(src, dst, i):
        return pltpu.make_async_copy(src, dst, in_sem.at[i])

    def settle(ref, sem, count):
        rest = ref.at[pl.ds(0, count)]
        pltpu.make_async_copy(rest, rest, sem).wait()

    barrier = pltpu.get_barrier_semaphore()

    def greet(j):
        pl.semaphore_signal(barrier, inc=1, device_id={"trade": j}, device_id_type=MESH)

    @pl.when(jnp.logical_or(is_first, is_hub))
    def _():
        each(greet, 0, n)

    @pl.when(is_second)
    def _():
        each(greet, quarter, n)

    @pl.when(is_late)
    def _():
        greet(hub)
        each(greet, near, n)

    own = local(factors, fact.at[me], 0)
    limit_copy = local(threshold, thr_s, 1)
    pairs = (
        (loadings, load_v),
        (basis_size, size_v),
        (netting_row, nrow_v),
        (set_ids, ids_v),
        (margin_start, marg_v),
        (trade_coef, coef_v),
    )
    copies = [local(src, dst, 2) for src, dst in pairs]
    for copy in (own, *copies, limit_copy):
        copy.start()
    own.wait()

    def gather(j):
        return pltpu.make_async_remote_copy(
            src_ref=fact.at[me],
            dst_ref=fact.at[me],
            send_sem=gs_sem,
            recv_sem=gr_sem.at[mine],
            device_id={"trade": j},
            device_id_type=MESH,
        )

    def relay(j, count):
        return pltpu.make_async_remote_copy(
            src_ref=fact.at[pl.ds(0, count)],
            dst_ref=fact.at[pl.ds(0, count)],
            send_sem=gs_sem,
            recv_sem=gr_sem.at[0],
            device_id={"trade": j},
            device_id_type=MESH,
        )

    @pl.when(is_first)
    def _():
        pl.semaphore_wait(barrier, quarter)
        gather(hub).start()
        each(lambda j: gather(j).start(), 0, quarter)

    @pl.when(is_second)
    def _():
        pl.semaphore_wait(barrier, near - 1)
        each(lambda j: gather(j).start(), 0, near)

    @pl.when(is_hub)
    def _():
        pl.semaphore_wait(barrier, n - 1)
        each(lambda j: gather(j).start(), 0, near)

    @pl.when(is_late)
    def _():
        pl.semaphore_wait(barrier, n - 1)
        each(lambda j: gather(j).start(), 0, n)

    for copy in copies:
        copy.wait()
    limit_copy.wait()
    tiled = (iota((F, LANES), 1) % F == iota((F, LANES), 0)).astype(f32).astype(bf16)
    diag = iota((DATES * K, LANES), 0) // K == iota((DATES * K, LANES), 1) // F
    rest = load_v[...]
    for i in range(3):
        piece = rest.astype(bf16)
        rest = rest - piece.astype(f32)
        wide = lax.dot_general(piece, tiled, (((0,), (0,)), ((), ())), preferred_element_type=f32)
        wide = jnp.concatenate([wide] * DATES, axis=0)
        split[i] = jnp.where(diag, wide, 0.0).astype(bf16)
    basis[...] = jnp.zeros(basis.shape, bf16)

    found = nrow_v[...] == iota((sets, sets), 0)
    owner_set = jnp.sum(jnp.where(found, iota((sets, sets), 1), 0).astype(f32), axis=1, keepdims=True)
    owner_set = owner_set.astype(jnp.int32)
    for c in range(slots // CHUNK):
        cut = slice(c * CHUNK, (c + 1) * CHUNK)
        onehot[:, cut] = (ids_v[:, cut] == owner_set).astype(f32).astype(bf16)

    for half in range(2):
        for i in range(LAG):
            held[half, :, i * paths : (i + 1) * paths] = marg_v[:, half * paths : (half + 1) * paths]

    live_now = live_count[0]
    slot_index = iota(size_v.shape, 0) * LANES + iota(size_v.shape, 1)
    used = jnp.where(slot_index < live_now, size_v[...], 0).astype(f32)
    basis_index = (iota((LANES, LANES), 1) % K).astype(f32)
    for c in range(slots // LANES):
        limit = jnp.broadcast_to(used[c : c + 1], (LANES, LANES)).T
        keep = basis_index < limit
        cut = slice(c * LANES, (c + 1) * LANES)
        for h in range(0, DATES * K, LANES):
            side = slice(h, h + LANES)
            coef_v[cut, side] = jnp.where(keep, coef_v[cut, side].astype(f32), 0.0).astype(bf16)

    def half_sums(half):
        for j in range(near):
            block = fact[half * near + j].astype(f32)
            for i in range(rep):
                at = i * paths + j * rows
                spread[at : at + rows] = block
        table = spread[...].astype(bf16)
        dims = (((1,), (1,)), ((), ()))
        loaded = lax.dot_general(split[2], table, dims, preferred_element_type=f32)
        loaded += lax.dot_general(split[1], table, dims, preferred_element_type=f32)
        loaded += lax.dot_general(split[0], table, dims, preferred_element_type=f32)
        bent = jnp.tanh(loaded)
        tall = rep * K
        pair = iota((tall, width), 0) // K == iota((tall, width), 1) // paths
        for j in range(DATES // rep):
            strip = jnp.where(pair, bent[j * tall : (j + 1) * tall], 0.0).astype(bf16)
            basis[j * tall : (j + 1) * tall, j * width : (j + 1) * width] = strip

        def block_sums(right):
            cuts = [slice(c * CHUNK, (c + 1) * CHUNK) for c in range(slots // CHUNK)]
            values = [jnp.dot(coef_v[cut], right, preferred_element_type=f32).astype(bf16) for cut in cuts]
            total = None
            for cut, value in zip(cuts, values):
                term = jnp.dot(onehot[:, cut], value, preferred_element_type=f32)
                total = term if total is None else total + term
            return total

        blocks = max(1, acc.shape[1] // COLS)
        if blocks == 1:
            acc[...] = block_sums(basis[...])
        else:

            def one(b, carry):
                side = pl.ds(pl.multiple_of(b * COLS, COLS), COLS)
                acc[:, side] = block_sums(basis[:, side])
                return carry

            lax.fori_loop(0, blocks, one, 0)
        for j in range(n):
            part[half, j] = acc[j * owned : (j + 1) * owned]

    def scatter(j, half, stage):
        return pltpu.make_async_remote_copy(
            src_ref=part.at[half, j],
            dst_ref=recv.at[half, me],
            send_sem=ss_sem.at[stage],
            recv_sem=sr_sem.at[half],
            device_id={"trade": j},
            device_id_type=MESH,
        )

    settle(fact, gr_sem.at[mine], near - 1)

    @pl.when(is_hub)
    def _():
        each(lambda j: relay(j, near).start(), near, n, among=False)
        each(lambda j: relay(j, quarter).start(), quarter, near)

    half_sums(mine)

    @pl.when(is_late)
    def _():
        each(lambda j: scatter(j, mine, 0).start(), 0, n)

    @pl.when(jnp.logical_not(is_late))
    def _():
        each(lambda j: scatter(j, mine, 0).start(), 0, near)

    settle(fact, gr_sem.at[1 - mine], near)

    @pl.when(jnp.logical_not(is_late))
    def _():
        each(lambda j: scatter(j, mine, 0).start(), near, n, among=False)

    half_sums(1 - mine)
    each(lambda j: scatter(j, 1 - mine, 1).start(), 0, n)
    for half in range(2):
        recv[half, me] = part[half, me]
    settle(recv.at[0], sr_sem.at[0], n - 1)
    settle(recv.at[1], sr_sem.at[1], n - 1)

    row_at = iota((owned, 1), 0)
    limits = jnp.zeros((owned, 1), f32)
    for r in range(owned):
        limits = jnp.where(row_at == r, thr_s[r], limits)
    first = LAG * paths
    result = jnp.zeros(out.shape, f32)
    lane_date = iota((owned, width), 1) // paths
    column = iota(out.shape, 1)
    short = jnp.zeros((owned, DATES * paths), f32)
    for half in range(2):
        netted = recv[half, 0]
        for j in range(1, n):
            netted = netted + recv[half, j]
        margin = jnp.maximum(netted[:, : (DATES - LAG) * paths] - limits, 0.0)
        collateral = jnp.concatenate([held[half], margin], axis=1)
        short = short + jnp.maximum(netted - collateral, 0.0)
    for j in range(DATES // rep):
        block = short[:, j * width : (j + 1) * width]
        for i in range(rep):
            own_date = jnp.where(lane_date == i, block, 0.0) if rep > 1 else block
            result = jnp.where(column == j * rep + i, jnp.sum(own_date, axis=1, keepdims=True), result)
    out[...] = result

    @pl.when(is_first)
    def _():
        settle(fact, gs_sem, quarter)

    @pl.when(jnp.logical_or(is_second, is_hub))
    def _():
        settle(fact, gs_sem, near - 1)

    @pl.when(is_hub)
    def _():
        each(lambda j: settle(fact, gs_sem, near), near, n, among=False)
        each(lambda j: settle(fact, gs_sem, quarter), quarter, near)

    @pl.when(is_late)
    def _():
        settle(fact, gs_sem, n - 1)

    settle(recv.at[0], ss_sem.at[0], n - 1)
    settle(recv.at[1], ss_sem.at[1], n - 1)


def stay(x):
    return pltpu.with_memory_space_constraint(x, pltpu.MemorySpace.HBM)


def body(n, factors, loadings, trade_coef, basis_size, set_ids, live_count, netting_row, threshold, margin_start):
    rows = factors.shape[0]
    paths = n * rows
    half = paths // 2
    rep = max(1, LANES // half)
    slots = trade_coef.shape[0]
    sets = netting_row.shape[0]
    owned = threshold.shape[0]
    wide = DATES * half
    hbm = pl.BlockSpec(memory_space=pltpu.MemorySpace.HBM)
    total = pl.pallas_call(
        functools.partial(kernel, n),
        out_shape=jax.ShapeDtypeStruct((owned, DATES), f32),
        in_specs=[hbm] * 5 + [pl.BlockSpec(memory_space=pltpu.SMEM)] + [hbm] * 3,
        out_specs=pl.BlockSpec(memory_space=pltpu.VMEM),
        scratch_shapes=[
            pltpu.VMEM((n, rows, DATES * F), bf16),
            pltpu.VMEM((F, K), f32),
            pltpu.VMEM((slots, DATES * K), bf16),
            pltpu.VMEM((slots // LANES, LANES), jnp.int32),
            pltpu.VMEM((1, slots), jnp.int32),
            pltpu.VMEM((1, sets), jnp.int32),
            pltpu.SMEM((owned,), f32),
            pltpu.VMEM((owned, paths), f32),
            pltpu.VMEM((3, DATES * K, DATES * F), bf16),
            pltpu.VMEM((sets, slots), bf16),
            pltpu.VMEM((rep * half, DATES * F), f32),
            pltpu.VMEM((DATES * K, wide), bf16),
            pltpu.VMEM((2, owned, LAG * half), f32),
            pltpu.VMEM((sets, wide), f32),
            pltpu.VMEM((2, n, owned, wide), f32),
            pltpu.VMEM((2, n, owned, wide), f32),
            pltpu.SemaphoreType.DMA((3,)),
            pltpu.SemaphoreType.DMA,
            pltpu.SemaphoreType.DMA((2,)),
            pltpu.SemaphoreType.DMA((2,)),
            pltpu.SemaphoreType.DMA((2,)),
        ],
        compiler_params=pltpu.CompilerParams(
            collective_id=0, has_side_effects=True, vmem_limit_bytes=48 * 2**20
        ),
    )(
        stay(factors),
        stay(loadings.T),
        stay(trade_coef),
        stay(basis_size.reshape(slots // LANES, LANES)),
        stay(set_ids.reshape(1, slots)),
        live_count,
        stay(netting_row.reshape(1, sets)),
        stay(threshold),
        stay(margin_start),
    )
    return total / paths


def solution(mesh):
    return jax.shard_map(
        functools.partial(body, mesh.shape["trade"]),
        mesh=mesh,
        in_specs=(
            P(("group", "trade"), None),
            P(),
            P(("group", "trade"), None),
            P(("group", "trade")),
            P(("group", "trade")),
            P(("group", "trade")),
            P("group"),
            P(("group", "trade")),
            P(("group", "trade"), None),
        ),
        out_specs=P(("group", "trade"), None),
        check_vma=False,
    )
```

```python
import functools

import jax
import jax.numpy as jnp
from jax import lax
from jax.experimental import pallas as pl
from jax.experimental.pallas import tpu as pltpu
from jax.sharding import PartitionSpec as P

F = 16
K = 32
DATES = 8
LAG = 2
LANES = 128
CHUNK = 256
COLS = 512
MESH = pl.DeviceIdType.MESH
f32 = jnp.float32
bf16 = jnp.bfloat16


def iota(shape, axis):
    return lax.broadcasted_iota(jnp.int32, shape, axis)


def kernel(
    n,
    factors,
    loadings,
    trade_coef,
    basis_size,
    set_ids,
    live_count,
    netting_row,
    threshold,
    margin_start,
    out,
    fact,
    load_v,
    coef_v,
    size_v,
    ids_v,
    nrow_v,
    thr_s,
    marg_v,
    split,
    onehot,
    spread,
    basis,
    held,
    acc,
    pooled,
    part,
    recv,
    in_sem,
    gs_sem,
    gr_sem,
    ss_sem,
    sr_sem,
):
    me = lax.axis_index("trade")
    rows = fact.shape[1]
    near = n // 2
    paths = near * rows
    rep = max(1, LANES // paths)
    width = rep * paths
    slots = coef_v.shape[0]
    owned = recv.shape[2]
    mine = lax.div(me, near)
    sets = n * owned

    quarter = n // 4
    hub = quarter + 1
    is_hub = me == hub
    is_late = me >= near
    is_last = me >= n - quarter
    is_first = me < quarter
    is_second = jnp.logical_and(jnp.logical_and(me >= quarter, me < near), me != hub)

    def each(step, lo, hi, among=True):
        def at(i):
            step(jnp.where(i >= me, i + 1, i) if among else i)

        count = hi - lo - 1 if among else hi - lo
        if n <= LANES // 4:
            for i in range(lo, lo + count):
                at(i)
        else:
            lax.fori_loop(lo, lo + count, lambda i, c: (at(i), c)[1], 0)

    def local(src, dst, i):
        return pltpu.make_async_copy(src, dst, in_sem.at[i])

    def settle(ref, sem, count):
        rest = ref.at[pl.ds(0, count)]
        pltpu.make_async_copy(rest, rest, sem).wait()

    barrier = pltpu.get_barrier_semaphore()

    def greet(j):
        pl.semaphore_signal(barrier, inc=1, device_id={"trade": j}, device_id_type=MESH)

    @pl.when(jnp.logical_or(is_first, is_hub))
    def _():
        each(greet, 0, n)

    @pl.when(is_second)
    def _():
        each(greet, quarter, n)

    @pl.when(is_late)
    def _():
        greet(hub)
        each(greet, near, n)

    own = local(factors, fact.at[me], 0)
    limit_copy = local(threshold, thr_s, 1)
    pairs = (
        (loadings, load_v),
        (basis_size, size_v),
        (netting_row, nrow_v),
        (set_ids, ids_v),
        (margin_start, marg_v),
        (trade_coef, coef_v),
    )
    copies = [local(src, dst, 2) for src, dst in pairs]
    for copy in (own, *copies, limit_copy):
        copy.start()
    own.wait()

    def gather(j):
        return pltpu.make_async_remote_copy(
            src_ref=fact.at[me],
            dst_ref=fact.at[me],
            send_sem=gs_sem,
            recv_sem=gr_sem.at[mine],
            device_id={"trade": j},
            device_id_type=MESH,
        )

    def relay(j, count):
        return pltpu.make_async_remote_copy(
            src_ref=fact.at[pl.ds(0, count)],
            dst_ref=fact.at[pl.ds(0, count)],
            send_sem=gs_sem,
            recv_sem=gr_sem.at[0],
            device_id={"trade": j},
            device_id_type=MESH,
        )

    @pl.when(is_first)
    def _():
        pl.semaphore_wait(barrier, quarter)
        gather(hub).start()
        each(lambda j: gather(j).start(), 0, quarter)

    @pl.when(is_second)
    def _():
        pl.semaphore_wait(barrier, near - 1)
        each(lambda j: gather(j).start(), 0, near)

    @pl.when(is_hub)
    def _():
        pl.semaphore_wait(barrier, n - 1)
        each(lambda j: gather(j).start(), 0, near)

    @pl.when(is_late)
    def _():
        pl.semaphore_wait(barrier, n - 1)
        each(lambda j: gather(j).start(), 0, n)

    for copy in copies:
        copy.wait()
    limit_copy.wait()
    tiled = (iota((F, LANES), 1) % F == iota((F, LANES), 0)).astype(f32).astype(bf16)
    diag = iota((DATES * K, LANES), 0) // K == iota((DATES * K, LANES), 1) // F
    rest = load_v[...]
    for i in range(3):
        piece = rest.astype(bf16)
        rest = rest - piece.astype(f32)
        wide = lax.dot_general(piece, tiled, (((0,), (0,)), ((), ())), preferred_element_type=f32)
        wide = jnp.concatenate([wide] * DATES, axis=0)
        split[i] = jnp.where(diag, wide, 0.0).astype(bf16)
    basis[...] = jnp.zeros(basis.shape, bf16)

    found = nrow_v[...] == iota((sets, sets), 0)
    owner_set = jnp.sum(jnp.where(found, iota((sets, sets), 1), 0).astype(f32), axis=1, keepdims=True)
    owner_set = owner_set.astype(jnp.int32)
    for c in range(slots // CHUNK):
        cut = slice(c * CHUNK, (c + 1) * CHUNK)
        onehot[:, cut] = (ids_v[:, cut] == owner_set).astype(f32).astype(bf16)

    for half in range(2):
        for i in range(LAG):
            held[half, :, i * paths : (i + 1) * paths] = marg_v[:, half * paths : (half + 1) * paths]

    live_now = live_count[0]
    slot_index = iota(size_v.shape, 0) * LANES + iota(size_v.shape, 1)
    used = jnp.where(slot_index < live_now, size_v[...], 0).astype(f32)
    basis_index = (iota((LANES, LANES), 1) % K).astype(f32)
    for c in range(slots // LANES):
        limit = jnp.broadcast_to(used[c : c + 1], (LANES, LANES)).T
        keep = basis_index < limit
        cut = slice(c * LANES, (c + 1) * LANES)
        for h in range(0, DATES * K, LANES):
            side = slice(h, h + LANES)
            coef_v[cut, side] = jnp.where(keep, coef_v[cut, side].astype(f32), 0.0).astype(bf16)

    @pl.when(is_last)
    def _():
        rest = None
        for c in range(slots // CHUNK):
            cut = slice(c * CHUNK, (c + 1) * CHUNK)
            term = jnp.dot(onehot[:, cut], coef_v[cut], preferred_element_type=f32)
            rest = term if rest is None else rest + term
        for i in range(3):
            piece = rest.astype(bf16)
            rest = rest - piece.astype(f32)
            pooled[i * sets : (i + 1) * sets] = piece

    def half_sums(half, pool=False):
        for j in range(near):
            block = fact[half * near + j].astype(f32)
            for i in range(rep):
                at = i * paths + j * rows
                spread[at : at + rows] = block
        table = spread[...].astype(bf16)
        dims = (((1,), (1,)), ((), ()))
        loaded = lax.dot_general(split[2], table, dims, preferred_element_type=f32)
        loaded += lax.dot_general(split[1], table, dims, preferred_element_type=f32)
        loaded += lax.dot_general(split[0], table, dims, preferred_element_type=f32)
        bent = jnp.tanh(loaded)
        tall = rep * K
        pair = iota((tall, width), 0) // K == iota((tall, width), 1) // paths
        for j in range(DATES // rep):
            strip = jnp.where(pair, bent[j * tall : (j + 1) * tall], 0.0).astype(bf16)
            basis[j * tall : (j + 1) * tall, j * width : (j + 1) * width] = strip

        def block_sums(right):
            if pool:
                thirds = jnp.dot(pooled[...], right, preferred_element_type=f32)
                return thirds[2 * sets :] + thirds[sets : 2 * sets] + thirds[:sets]
            cuts = [slice(c * CHUNK, (c + 1) * CHUNK) for c in range(slots // CHUNK)]
            values = [jnp.dot(coef_v[cut], right, preferred_element_type=f32).astype(bf16) for cut in cuts]
            total = None
            for cut, value in zip(cuts, values):
                term = jnp.dot(onehot[:, cut], value, preferred_element_type=f32)
                total = term if total is None else total + term
            return total

        blocks = max(1, acc.shape[1] // COLS)
        if blocks == 1:
            acc[...] = block_sums(basis[...])
        else:

            def one(b, carry):
                side = pl.ds(pl.multiple_of(b * COLS, COLS), COLS)
                acc[:, side] = block_sums(basis[:, side])
                return carry

            lax.fori_loop(0, blocks, one, 0)
        for j in range(n):
            part[half, j] = acc[j * owned : (j + 1) * owned]

    def scatter(j, half, stage):
        return pltpu.make_async_remote_copy(
            src_ref=part.at[half, j],
            dst_ref=recv.at[half, me],
            send_sem=ss_sem.at[stage],
            recv_sem=sr_sem.at[half],
            device_id={"trade": j},
            device_id_type=MESH,
        )

    settle(fact, gr_sem.at[mine], near - 1)

    @pl.when(is_hub)
    def _():
        each(lambda i: relay(n - 1 - i, near).start(), 0, near, among=False)
        each(lambda j: relay(j, quarter).start(), quarter, near)

    half_sums(mine)

    @pl.when(is_late)
    def _():
        each(lambda j: scatter(j, mine, 0).start(), 0, n)

    @pl.when(jnp.logical_not(is_late))
    def _():
        each(lambda j: scatter(j, mine, 0).start(), 0, near)

    settle(fact, gr_sem.at[1 - mine], near)

    @pl.when(jnp.logical_not(is_late))
    def _():
        each(lambda j: scatter(j, mine, 0).start(), near, n, among=False)


    @pl.when(is_last)
    def _():
        half_sums(1 - mine, pool=True)

    @pl.when(jnp.logical_not(is_last))
    def _():
        half_sums(1 - mine)

    each(lambda j: scatter(j, 1 - mine, 1).start(), 0, n)
    for half in range(2):
        recv[half, me] = part[half, me]
    settle(recv.at[0], sr_sem.at[0], n - 1)
    settle(recv.at[1], sr_sem.at[1], n - 1)

    row_at = iota((owned, 1), 0)
    limits = jnp.zeros((owned, 1), f32)
    for r in range(owned):
        limits = jnp.where(row_at == r, thr_s[r], limits)
    first = LAG * paths
    result = jnp.zeros(out.shape, f32)
    lane_date = iota((owned, width), 1) // paths
    column = iota(out.shape, 1)
    short = jnp.zeros((owned, DATES * paths), f32)
    for half in range(2):
        netted = recv[half, 0]
        for j in range(1, n):
            netted = netted + recv[half, j]
        margin = jnp.maximum(netted[:, : (DATES - LAG) * paths] - limits, 0.0)
        collateral = jnp.concatenate([held[half], margin], axis=1)
        short = short + jnp.maximum(netted - collateral, 0.0)
    for j in range(DATES // rep):
        block = short[:, j * width : (j + 1) * width]
        for i in range(rep):
            own_date = jnp.where(lane_date == i, block, 0.0) if rep > 1 else block
            result = jnp.where(column == j * rep + i, jnp.sum(own_date, axis=1, keepdims=True), result)
    out[...] = result

    @pl.when(is_first)
    def _():
        settle(fact, gs_sem, quarter)

    @pl.when(jnp.logical_or(is_second, is_hub))
    def _():
        settle(fact, gs_sem, near - 1)

    @pl.when(is_hub)
    def _():
        each(lambda j: settle(fact, gs_sem, near), near, n, among=False)
        each(lambda j: settle(fact, gs_sem, quarter), quarter, near)

    @pl.when(is_late)
    def _():
        settle(fact, gs_sem, n - 1)

    settle(recv.at[0], ss_sem.at[0], n - 1)
    settle(recv.at[1], ss_sem.at[1], n - 1)


def stay(x):
    return pltpu.with_memory_space_constraint(x, pltpu.MemorySpace.HBM)


def body(n, factors, loadings, trade_coef, basis_size, set_ids, live_count, netting_row, threshold, margin_start):
    rows = factors.shape[0]
    paths = n * rows
    half = paths // 2
    rep = max(1, LANES // half)
    slots = trade_coef.shape[0]
    sets = netting_row.shape[0]
    owned = threshold.shape[0]
    wide = DATES * half
    hbm = pl.BlockSpec(memory_space=pltpu.MemorySpace.HBM)
    total = pl.pallas_call(
        functools.partial(kernel, n),
        out_shape=jax.ShapeDtypeStruct((owned, DATES), f32),
        in_specs=[hbm] * 5 + [pl.BlockSpec(memory_space=pltpu.SMEM)] + [hbm] * 3,
        out_specs=pl.BlockSpec(memory_space=pltpu.VMEM),
        scratch_shapes=[
            pltpu.VMEM((n, rows, DATES * F), bf16),
            pltpu.VMEM((F, K), f32),
            pltpu.VMEM((slots, DATES * K), bf16),
            pltpu.VMEM((slots // LANES, LANES), jnp.int32),
            pltpu.VMEM((1, slots), jnp.int32),
            pltpu.VMEM((1, sets), jnp.int32),
            pltpu.SMEM((owned,), f32),
            pltpu.VMEM((owned, paths), f32),
            pltpu.VMEM((3, DATES * K, DATES * F), bf16),
            pltpu.VMEM((sets, slots), bf16),
            pltpu.VMEM((rep * half, DATES * F), f32),
            pltpu.VMEM((DATES * K, wide), bf16),
            pltpu.VMEM((2, owned, LAG * half), f32),
            pltpu.VMEM((sets, wide), f32),
            pltpu.VMEM((3 * sets, DATES * K), bf16),
            pltpu.VMEM((2, n, owned, wide), f32),
            pltpu.VMEM((2, n, owned, wide), f32),
            pltpu.SemaphoreType.DMA((3,)),
            pltpu.SemaphoreType.DMA,
            pltpu.SemaphoreType.DMA((2,)),
            pltpu.SemaphoreType.DMA((2,)),
            pltpu.SemaphoreType.DMA((2,)),
        ],
        compiler_params=pltpu.CompilerParams(
            collective_id=0, has_side_effects=True, vmem_limit_bytes=48 * 2**20
        ),
    )(
        stay(factors),
        stay(loadings.T),
        stay(trade_coef),
        stay(basis_size.reshape(slots // LANES, LANES)),
        stay(set_ids.reshape(1, slots)),
        live_count,
        stay(netting_row.reshape(1, sets)),
        stay(threshold),
        stay(margin_start),
    )
    return total / paths


def solution(mesh):
    return jax.shard_map(
        functools.partial(body, mesh.shape["trade"]),
        mesh=mesh,
        in_specs=(
            P(("group", "trade"), None),
            P(),
            P(("group", "trade"), None),
            P(("group", "trade")),
            P(("group", "trade")),
            P(("group", "trade")),
            P("group"),
            P(("group", "trade")),
            P(("group", "trade"), None),
        ),
        out_specs=P(("group", "trade"), None),
        check_vma=False,
    )
```

```python
import functools

import jax
import jax.numpy as jnp
from jax import lax
from jax.experimental import pallas as pl
from jax.experimental.pallas import tpu as pltpu
from jax.sharding import PartitionSpec as P

F = 16
K = 32
DATES = 8
LAG = 2
LANES = 128
CHUNK = 256
COLS = 512
MESH = pl.DeviceIdType.MESH
f32 = jnp.float32
bf16 = jnp.bfloat16


def iota(shape, axis):
    return lax.broadcasted_iota(jnp.int32, shape, axis)


def kernel(
    n,
    factors,
    loadings,
    trade_coef,
    basis_size,
    set_ids,
    live_count,
    netting_row,
    threshold,
    margin_start,
    out,
    fact,
    load_v,
    coef_v,
    size_v,
    ids_v,
    nrow_v,
    thr_s,
    marg_v,
    split,
    onehot,
    spread,
    basis,
    held,
    acc,
    part,
    recv,
    part_c,
    recv_c,
    in_sem,
    gs_sem,
    gr_sem,
    pair_sem,
    ss_sem,
    sr_sem,
    cs_sem,
    cr_sem,
    ready,
):
    me = lax.axis_index("trade")
    rows = fact.shape[1]
    near = n // 2
    paths = near * rows
    rep = max(1, LANES // paths)
    width = rep * paths
    slots = coef_v.shape[0]
    owned = recv.shape[2]
    mine = lax.div(me, near)
    sets = n * owned

    quarter = n // 4
    hub = quarter + 1
    is_hub = me == hub
    is_late = me >= near
    last = n - quarter
    odd = lax.rem(me, 2) == 1
    is_last = me >= last
    is_even = jnp.logical_and(jnp.logical_and(is_late, me < last), jnp.logical_not(odd))
    is_odd = jnp.logical_and(jnp.logical_and(is_late, me < last), odd)
    pool = n - recv_c.shape[0]
    is_early = jnp.logical_not(is_late)

    def each(step, lo, hi, among=True):
        def at(i):
            step(jnp.where(i >= me, i + 1, i) if among else i)

        count = hi - lo - 1 if among else hi - lo
        if n <= LANES // 4:
            for i in range(lo, lo + count):
                at(i)
        else:
            lax.fori_loop(lo, lo + count, lambda i, c: (at(i), c)[1], 0)

    def local(src, dst, i):
        return pltpu.make_async_copy(src, dst, in_sem.at[i])

    def settle(ref, sem, count):
        rest = ref.at[pl.ds(0, count)]
        pltpu.make_async_copy(rest, rest, sem).wait()

    barrier = pltpu.get_barrier_semaphore()

    def greet(j):
        pl.semaphore_signal(barrier, inc=1, device_id={"trade": j}, device_id_type=MESH)

    @pl.when(is_early)
    def _():
        each(greet, 0, n)

    @pl.when(jnp.logical_or(is_even, is_odd))
    def _():
        greet(hub)
        each(greet, near, n)

    @pl.when(is_last)
    def _():
        greet(hub)
        each(lambda i: greet(near + 1 + 2 * i), 0, quarter // 2, among=False)
        each(greet, last, n)

    own = local(factors, fact.at[me], 0)
    limit_copy = local(threshold, thr_s, 1)
    pairs = (
        (loadings, load_v),
        (basis_size, size_v),
        (netting_row, nrow_v),
        (set_ids, ids_v),
        (margin_start, marg_v),
        (trade_coef, coef_v),
    )
    copies = [local(src, dst, 2) for src, dst in pairs]
    for copy in (own, *copies, limit_copy):
        copy.start()
    own.wait()

    def gather(j):
        return pltpu.make_async_remote_copy(
            src_ref=fact.at[me],
            dst_ref=fact.at[me],
            send_sem=gs_sem,
            recv_sem=gr_sem.at[mine],
            device_id={"trade": j},
            device_id_type=MESH,
        )

    def relay(j):
        return pltpu.make_async_remote_copy(
            src_ref=fact.at[pl.ds(0, near)],
            dst_ref=fact.at[pl.ds(0, near)],
            send_sem=gs_sem,
            recv_sem=gr_sem.at[0],
            device_id={"trade": j},
            device_id_type=MESH,
        )

    def report():
        pl.semaphore_signal(ready, inc=1, device_id={"trade": hub}, device_id_type=MESH)

    @pl.when(jnp.logical_and(is_early, me != hub))
    def _():
        pl.semaphore_wait(barrier, near - 1)
        report()
        each(lambda j: gather(j).start(), 0, near)

    @pl.when(is_hub)
    def _():
        pl.semaphore_wait(ready, near - 1)
        each(lambda j: gather(j).start(), 0, near)

    def to_partner():
        return pltpu.make_async_remote_copy(
            src_ref=fact.at[me],
            dst_ref=fact.at[me],
            send_sem=gs_sem,
            recv_sem=pair_sem,
            device_id={"trade": me + 1},
            device_id_type=MESH,
        )

    def pair(j):
        both = pl.ds(me - 1, 2)
        return pltpu.make_async_remote_copy(
            src_ref=fact.at[both],
            dst_ref=fact.at[both],
            send_sem=gs_sem,
            recv_sem=gr_sem.at[1],
            device_id={"trade": j},
            device_id_type=MESH,
        )

    @pl.when(is_even)
    def _():
        pl.semaphore_wait(barrier, last - 1)
        to_partner().start()

        def send(j):
            @pl.when(j != me + 1)
            def _():
                gather(j).start()

        each(send, 0, last)

    @pl.when(is_odd)
    def _():
        pl.semaphore_wait(barrier, n - 1)
        settle(fact, pair_sem, 1)
        each(lambda i: pair(n - 1 - i).start(), 0, quarter, among=False)
        each(lambda j: gather(j).start(), 0, last)

    @pl.when(is_last)
    def _():
        pl.semaphore_wait(barrier, n - 1)
        each(lambda j: gather(j).start(), 0, n)

    for copy in copies:
        copy.wait()
    limit_copy.wait()
    tiled = (iota((F, LANES), 1) % F == iota((F, LANES), 0)).astype(f32).astype(bf16)
    diag = iota((DATES * K, LANES), 0) // K == iota((DATES * K, LANES), 1) // F
    rest = load_v[...]
    for i in range(3):
        piece = rest.astype(bf16)
        rest = rest - piece.astype(f32)
        wide = lax.dot_general(piece, tiled, (((0,), (0,)), ((), ())), preferred_element_type=f32)
        wide = jnp.concatenate([wide] * DATES, axis=0)
        split[i] = jnp.where(diag, wide, 0.0).astype(bf16)
    basis[...] = jnp.zeros(basis.shape, bf16)

    found = nrow_v[...] == iota((sets, sets), 0)
    owner_set = jnp.sum(jnp.where(found, iota((sets, sets), 1), 0).astype(f32), axis=1, keepdims=True)
    owner_set = owner_set.astype(jnp.int32)
    for c in range(slots // CHUNK):
        cut = slice(c * CHUNK, (c + 1) * CHUNK)
        onehot[:, cut] = (ids_v[:, cut] == owner_set).astype(f32).astype(bf16)

    for half in range(2):
        for i in range(LAG):
            held[half, :, i * paths : (i + 1) * paths] = marg_v[:, half * paths : (half + 1) * paths]

    live_now = live_count[0]
    slot_index = iota(size_v.shape, 0) * LANES + iota(size_v.shape, 1)
    used = jnp.where(slot_index < live_now, size_v[...], 0).astype(f32)
    basis_index = (iota((LANES, LANES), 1) % K).astype(f32)
    for c in range(slots // LANES):
        limit = jnp.broadcast_to(used[c : c + 1], (LANES, LANES)).T
        keep = basis_index < limit
        cut = slice(c * LANES, (c + 1) * LANES)
        for h in range(0, DATES * K, LANES):
            side = slice(h, h + LANES)
            coef_v[cut, side] = jnp.where(keep, coef_v[cut, side].astype(f32), 0.0).astype(bf16)

    def pass_coefs(j):
        return pltpu.make_async_remote_copy(
            src_ref=part_c.at[j],
            dst_ref=recv_c.at[me - pool],
            send_sem=cs_sem,
            recv_sem=cr_sem,
            device_id={"trade": j},
            device_id_type=MESH,
        )

    @pl.when(is_late)
    def _():
        total = None
        for c in range(slots // CHUNK):
            cut = slice(c * CHUNK, (c + 1) * CHUNK)
            term = jnp.dot(onehot[:, cut], coef_v[cut], preferred_element_type=f32)
            total = term if total is None else total + term
        for j in range(n):
            part_c[j] = total[j * owned : (j + 1) * owned]
        each(lambda j: pass_coefs(j).start(), 0, near, among=False)
        recv_c[me - pool] = part_c[me]

    def make_basis(half):
        for j in range(near):
            block = fact[half * near + j].astype(f32)
            for i in range(rep):
                at = i * paths + j * rows
                spread[at : at + rows] = block
        table = spread[...].astype(bf16)
        dims = (((1,), (1,)), ((), ()))
        loaded = lax.dot_general(split[2], table, dims, preferred_element_type=f32)
        loaded += lax.dot_general(split[1], table, dims, preferred_element_type=f32)
        loaded += lax.dot_general(split[0], table, dims, preferred_element_type=f32)
        bent = jnp.tanh(loaded)
        tall = rep * K
        pair = iota((tall, width), 0) // K == iota((tall, width), 1) // paths
        for j in range(DATES // rep):
            strip = jnp.where(pair, bent[j * tall : (j + 1) * tall], 0.0).astype(bf16)
            basis[half, j * tall : (j + 1) * tall, j * width : (j + 1) * width] = strip

    def half_sums(half):
        make_basis(half)

        def block_sums(right):
            cuts = [slice(c * CHUNK, (c + 1) * CHUNK) for c in range(slots // CHUNK)]
            values = [jnp.dot(coef_v[cut], right, preferred_element_type=f32).astype(bf16) for cut in cuts]
            total = None
            for cut, value in zip(cuts, values):
                term = jnp.dot(onehot[:, cut], value, preferred_element_type=f32)
                total = term if total is None else total + term
            return total

        blocks = max(1, acc.shape[1] // COLS)
        if blocks == 1:
            acc[...] = block_sums(basis[half])
        else:

            def one(b, carry):
                side = pl.ds(pl.multiple_of(b * COLS, COLS), COLS)
                acc[:, side] = block_sums(basis[half, :, side])
                return carry

            lax.fori_loop(0, blocks, one, 0)
        for j in range(n):
            part[half, j] = acc[j * owned : (j + 1) * owned]

    def scatter(j, half, stage):
        return pltpu.make_async_remote_copy(
            src_ref=part.at[half, j],
            dst_ref=recv.at[half, me],
            send_sem=ss_sem.at[stage],
            recv_sem=sr_sem.at[half],
            device_id={"trade": j},
            device_id_type=MESH,
        )

    @pl.when(is_hub)
    def _():
        pl.semaphore_wait(barrier, n - 1)

    @pl.when(is_odd)
    def _():
        settle(fact, gr_sem.at[1], near - 2)

    @pl.when(jnp.logical_not(is_odd))
    def _():
        settle(fact, gr_sem.at[mine], near - 1)

    @pl.when(is_hub)
    def _():
        each(lambda i: relay(n - 1 - i).start(), 0, near, among=False)
    half_sums(mine)

    @pl.when(is_late)
    def _():
        each(lambda j: scatter(j, mine, 0).start(), 0, n)
        each(lambda j: pass_coefs(j).start(), near, n)

    @pl.when(is_early)
    def _():
        each(lambda j: scatter(j, mine, 0).start(), 0, near)

    settle(fact, gr_sem.at[1 - mine], near)

    @pl.when(is_early)
    def _():
        each(lambda j: scatter(j, mine, 0).start(), near, n, among=False)


    @pl.when(is_early)
    def _():
        half_sums(1 - mine)
        each(lambda j: scatter(j, 1 - mine, 1).start(), 0, n)
        recv[1 - mine, me] = part[1 - mine, me]
        settle(recv_c, cr_sem, n - pool)

    @pl.when(is_late)
    def _():
        make_basis(1 - mine)
        settle(recv_c, cr_sem, n - pool - 1)

    recv[mine, me] = part[mine, me]
    rest = recv_c[0]
    for j in range(1, n - pool):
        rest = rest + recv_c[j]
    pieces = []
    for i in range(3):
        pieces.append(rest.astype(bf16).astype(f32))
        rest = rest - pieces[i]
    stack = jnp.concatenate(pieces, axis=0).astype(bf16)
    thirds = jnp.dot(stack, basis[0], preferred_element_type=f32)
    recv[0, pool] = thirds[2 * owned :] + thirds[owned : 2 * owned] + thirds[:owned]
    for j in range(pool + 1, n):
        recv[0, j] = jnp.zeros(recv.shape[2:], f32)

    row_at = iota((owned, 1), 0)
    limits = jnp.zeros((owned, 1), f32)
    for r in range(owned):
        limits = jnp.where(row_at == r, thr_s[r], limits)
    first = LAG * paths
    result = jnp.zeros(out.shape, f32)
    lane_date = iota((owned, width), 1) // paths
    column = iota(out.shape, 1)

    def shortfall(half):
        netted = recv[half, 0]
        for j in range(1, n):
            netted = netted + recv[half, j]
        margin = jnp.maximum(netted[:, : (DATES - LAG) * paths] - limits, 0.0)
        collateral = jnp.concatenate([held[half], margin], axis=1)
        return jnp.maximum(netted - collateral, 0.0)

    @pl.when(is_early)
    def _():
        settle(recv.at[0], sr_sem.at[0], pool - 1)

    @pl.when(is_late)
    def _():
        settle(recv.at[0], sr_sem.at[0], pool)

    short = shortfall(0)
    settle(recv.at[1], sr_sem.at[1], n - 1)
    short = short + shortfall(1)
    for j in range(DATES // rep):
        block = short[:, j * width : (j + 1) * width]
        for i in range(rep):
            own_date = jnp.where(lane_date == i, block, 0.0) if rep > 1 else block
            result = jnp.where(column == j * rep + i, jnp.sum(own_date, axis=1, keepdims=True), result)
    out[...] = result

    @pl.when(is_early)
    def _():
        settle(fact, gs_sem, near - 1)

    @pl.when(is_hub)
    def _():
        each(lambda j: settle(fact, gs_sem, near), near, n, among=False)

    @pl.when(jnp.logical_or(is_even, is_odd))
    def _():
        settle(fact, gs_sem, last - 1)

    @pl.when(is_odd)
    def _():
        settle(fact, gs_sem, 2 * quarter)

    @pl.when(is_last)
    def _():
        settle(fact, gs_sem, n - 1)

    settle(recv.at[0], ss_sem.at[0], n - 1)

    @pl.when(is_early)
    def _():
        settle(recv.at[1], ss_sem.at[1], n - 1)

    @pl.when(is_late)
    def _():
        settle(part_c, cs_sem, n - 1)


def stay(x):
    return pltpu.with_memory_space_constraint(x, pltpu.MemorySpace.HBM)


def body(n, factors, loadings, trade_coef, basis_size, set_ids, live_count, netting_row, threshold, margin_start):
    rows = factors.shape[0]
    paths = n * rows
    half = paths // 2
    rep = max(1, LANES // half)
    slots = trade_coef.shape[0]
    sets = netting_row.shape[0]
    owned = threshold.shape[0]
    wide = DATES * half
    hbm = pl.BlockSpec(memory_space=pltpu.MemorySpace.HBM)
    total = pl.pallas_call(
        functools.partial(kernel, n),
        out_shape=jax.ShapeDtypeStruct((owned, DATES), f32),
        in_specs=[hbm] * 5 + [pl.BlockSpec(memory_space=pltpu.SMEM)] + [hbm] * 3,
        out_specs=pl.BlockSpec(memory_space=pltpu.VMEM),
        scratch_shapes=[
            pltpu.VMEM((n, rows, DATES * F), bf16),
            pltpu.VMEM((F, K), f32),
            pltpu.VMEM((slots, DATES * K), bf16),
            pltpu.VMEM((slots // LANES, LANES), jnp.int32),
            pltpu.VMEM((1, slots), jnp.int32),
            pltpu.VMEM((1, sets), jnp.int32),
            pltpu.SMEM((owned,), f32),
            pltpu.VMEM((owned, paths), f32),
            pltpu.VMEM((3, DATES * K, DATES * F), bf16),
            pltpu.VMEM((sets, slots), bf16),
            pltpu.VMEM((rep * half, DATES * F), f32),
            pltpu.VMEM((2, DATES * K, wide), bf16),
            pltpu.VMEM((2, owned, LAG * half), f32),
            pltpu.VMEM((sets, wide), f32),
            pltpu.VMEM((2, n, owned, wide), f32),
            pltpu.VMEM((2, n, owned, wide), f32),
            pltpu.VMEM((n, owned, DATES * K), f32),
            pltpu.VMEM((n // 2, owned, DATES * K), f32),
            pltpu.SemaphoreType.DMA((3,)),
            pltpu.SemaphoreType.DMA,
            pltpu.SemaphoreType.DMA((2,)),
            pltpu.SemaphoreType.DMA,
            pltpu.SemaphoreType.DMA((2,)),
            pltpu.SemaphoreType.DMA((2,)),
            pltpu.SemaphoreType.DMA,
            pltpu.SemaphoreType.DMA,
            pltpu.SemaphoreType.REGULAR,
        ],
        compiler_params=pltpu.CompilerParams(
            collective_id=0, has_side_effects=True, vmem_limit_bytes=48 * 2**20
        ),
    )(
        stay(factors),
        stay(loadings.T),
        stay(trade_coef),
        stay(basis_size.reshape(slots // LANES, LANES)),
        stay(set_ids.reshape(1, slots)),
        live_count,
        stay(netting_row.reshape(1, sets)),
        stay(threshold),
        stay(margin_start),
    )
    return total / paths


def solution(mesh):
    return jax.shard_map(
        functools.partial(body, mesh.shape["trade"]),
        mesh=mesh,
        in_specs=(
            P(("group", "trade"), None),
            P(),
            P(("group", "trade"), None),
            P(("group", "trade")),
            P(("group", "trade")),
            P(("group", "trade")),
            P("group"),
            P(("group", "trade")),
            P(("group", "trade"), None),
        ),
        out_specs=P(("group", "trade"), None),
        check_vma=False,
    )
```

```python
import functools

import jax
import jax.numpy as jnp
from jax import lax
from jax.experimental import pallas as pl
from jax.experimental.pallas import tpu as pltpu
from jax.sharding import PartitionSpec as P

F = 16
K = 32
DATES = 8
LAG = 2
LANES = 128
CHUNK = 256
COLS = 512
MESH = pl.DeviceIdType.MESH
f32 = jnp.float32
bf16 = jnp.bfloat16


def iota(shape, axis):
    return lax.broadcasted_iota(jnp.int32, shape, axis)


def kernel(
    n,
    factors,
    loadings,
    trade_coef,
    basis_size,
    set_ids,
    live_count,
    netting_row,
    threshold,
    margin_start,
    out,
    fact,
    load_v,
    coef_v,
    size_v,
    ids_v,
    nrow_v,
    thr_s,
    marg_v,
    split,
    onehot,
    spread,
    basis,
    held,
    acc,
    part,
    recv,
    part_c,
    recv_c,
    in_sem,
    gs_sem,
    gr_sem,
    pair_sem,
    ss_sem,
    sr_sem,
    cs_sem,
    cr_sem,
    ready,
):
    me = lax.axis_index("trade")
    rows = fact.shape[1]
    near = n // 2
    paths = near * rows
    rep = max(1, LANES // paths)
    width = rep * paths
    slots = coef_v.shape[0]
    owned = recv.shape[2]
    mine = lax.div(me, near)
    sets = n * owned

    quarter = n // 4
    hub = quarter + 1
    is_hub = me == hub
    is_late = me >= near
    slow = near + 1
    odd = lax.rem(me, 2) == 1
    is_even = jnp.logical_and(is_late, jnp.logical_not(odd))
    is_odd = jnp.logical_and(is_late, odd)
    is_final = me >= n - 2
    pool = n - recv_c.shape[0]
    is_early = jnp.logical_not(is_late)

    def each(step, lo, hi, among=True):
        def at(i):
            step(jnp.where(i >= me, i + 1, i) if among else i)

        count = hi - lo - 1 if among else hi - lo
        if n <= LANES // 4:
            for i in range(lo, lo + count):
                at(i)
        else:
            lax.fori_loop(lo, lo + count, lambda i, c: (at(i), c)[1], 0)

    def local(src, dst, i):
        return pltpu.make_async_copy(src, dst, in_sem.at[i])

    def settle(ref, sem, count):
        rest = ref.at[pl.ds(0, count)]
        pltpu.make_async_copy(rest, rest, sem).wait()

    barrier = pltpu.get_barrier_semaphore()

    def greet(j):
        pl.semaphore_signal(barrier, inc=1, device_id={"trade": j}, device_id_type=MESH)

    @pl.when(is_early)
    def _():
        each(greet, 0, near)

    def each_odd(step):
        def at(i):
            j = near + 1 + 2 * i

            @pl.when(j != me)
            def _():
                step(j)

        if n <= LANES // 4:
            for i in range(quarter - 1, -1, -1):
                at(i)
        else:
            lax.fori_loop(0, quarter, lambda i, c: (at(quarter - 1 - i), c)[1], 0)

    @pl.when(is_odd)
    def _():
        greet(me - 1)

    each_odd(greet)

    own = local(factors, fact.at[me], 0)
    limit_copy = local(threshold, thr_s, 1)
    pairs = (
        (loadings, load_v),
        (basis_size, size_v),
        (netting_row, nrow_v),
        (set_ids, ids_v),
        (margin_start, marg_v),
        (trade_coef, coef_v),
    )
    copies = [local(src, dst, 2) for src, dst in pairs]
    for copy in (own, *copies, limit_copy):
        copy.start()
    def gather(j, lane=None):
        return pltpu.make_async_remote_copy(
            src_ref=fact.at[me],
            dst_ref=fact.at[me],
            send_sem=gs_sem,
            recv_sem=gr_sem.at[mine if lane is None else lane],
            device_id={"trade": j},
            device_id_type=MESH,
        )

    def relay(j):
        return pltpu.make_async_remote_copy(
            src_ref=fact.at[pl.ds(0, near)],
            dst_ref=fact.at[pl.ds(0, near)],
            send_sem=gs_sem,
            recv_sem=gr_sem.at[0],
            device_id={"trade": j},
            device_id_type=MESH,
        )

    @pl.when(is_early)
    def _():
        own.wait()
        pl.semaphore_wait(barrier, near - 1)
        each(lambda j: gather(j).start(), 0, near)

    def to_partner():
        return pltpu.make_async_remote_copy(
            src_ref=factors,
            dst_ref=fact.at[me],
            send_sem=gs_sem,
            recv_sem=pair_sem,
            device_id={"trade": me + 1},
            device_id_type=MESH,
        )

    def pair(j):
        both = pl.ds(me - 1, 2)
        return pltpu.make_async_remote_copy(
            src_ref=fact.at[both],
            dst_ref=fact.at[both],
            send_sem=gs_sem,
            recv_sem=gr_sem.at[jnp.where(jnp.logical_and(me == slow, j >= n - 2), 2, 1)],
            device_id={"trade": j},
            device_id_type=MESH,
        )

    @pl.when(is_even)
    def _():
        pl.semaphore_wait(barrier, 1)
        to_partner().start()
        own.wait()

    @pl.when(is_odd)
    def _():
        own.wait()
        pl.semaphore_wait(barrier, n - 1)

        @pl.when(me == slow)
        def _():
            pl.semaphore_signal(ready, inc=1, device_id={"trade": hub}, device_id_type=MESH)

        gather(me - 1, 3).start()
        settle(fact, pair_sem, 1)
        each_odd(lambda j: pair(j - 1).start())
        each_odd(lambda j: pair(j).start())
        each(lambda j: pair(j).start(), 0, near, among=False)

    for copy in copies:
        copy.wait()
    limit_copy.wait()
    tiled = (iota((F, LANES), 1) % F == iota((F, LANES), 0)).astype(f32).astype(bf16)
    diag = iota((DATES * K, LANES), 0) // K == iota((DATES * K, LANES), 1) // F
    rest = load_v[...]
    for i in range(3):
        piece = rest.astype(bf16)
        rest = rest - piece.astype(f32)
        wide = lax.dot_general(piece, tiled, (((0,), (0,)), ((), ())), preferred_element_type=f32)
        wide = jnp.concatenate([wide] * DATES, axis=0)
        split[i] = jnp.where(diag, wide, 0.0).astype(bf16)
    basis[...] = jnp.zeros(basis.shape, bf16)

    found = nrow_v[...] == iota((sets, sets), 0)
    owner_set = jnp.sum(jnp.where(found, iota((sets, sets), 1), 0).astype(f32), axis=1, keepdims=True)
    owner_set = owner_set.astype(jnp.int32)
    for c in range(slots // CHUNK):
        cut = slice(c * CHUNK, (c + 1) * CHUNK)
        onehot[:, cut] = (ids_v[:, cut] == owner_set).astype(f32).astype(bf16)

    for half in range(2):
        for i in range(LAG):
            held[half, :, i * paths : (i + 1) * paths] = marg_v[:, half * paths : (half + 1) * paths]

    live_now = live_count[0]
    slot_index = iota(size_v.shape, 0) * LANES + iota(size_v.shape, 1)
    used = jnp.where(slot_index < live_now, size_v[...], 0).astype(f32)
    basis_index = (iota((LANES, LANES), 1) % K).astype(f32)
    for c in range(slots // LANES):
        limit = jnp.broadcast_to(used[c : c + 1], (LANES, LANES)).T
        keep = basis_index < limit
        cut = slice(c * LANES, (c + 1) * LANES)
        for h in range(0, DATES * K, LANES):
            side = slice(h, h + LANES)
            coef_v[cut, side] = jnp.where(keep, coef_v[cut, side].astype(f32), 0.0).astype(bf16)

    def pass_coefs(j):
        return pltpu.make_async_remote_copy(
            src_ref=part_c.at[j],
            dst_ref=recv_c.at[me - pool],
            send_sem=cs_sem,
            recv_sem=cr_sem,
            device_id={"trade": j},
            device_id_type=MESH,
        )

    @pl.when(is_late)
    def _():
        total = None
        for c in range(slots // CHUNK):
            cut = slice(c * CHUNK, (c + 1) * CHUNK)
            term = jnp.dot(onehot[:, cut], coef_v[cut], preferred_element_type=f32)
            total = term if total is None else total + term
        for j in range(n):
            part_c[j] = total[j * owned : (j + 1) * owned]

        @pl.when(is_even)
        def _():
            settle(fact, gr_sem.at[3], 1)

        each(lambda j: pass_coefs(j).start(), 0, near, among=False)
        recv_c[me - pool] = part_c[me]

    def make_basis(half, hold=False):
        for j in range(near):

            def fill(j=j):
                block = fact[half * near + j].astype(f32)
                for i in range(rep):
                    at = i * paths + j * rows
                    spread[at : at + rows] = block

            if hold and j < 2:
                pl.when(jnp.logical_not(is_final))(fill)

                @pl.when(is_final)
                def _():
                    for i in range(rep):
                        at = i * paths + j * rows
                        spread[at : at + rows] = jnp.zeros((rows, spread.shape[1]), f32)

            else:
                fill()
        table = spread[...].astype(bf16)
        dims = (((1,), (1,)), ((), ()))
        loaded = lax.dot_general(split[2], table, dims, preferred_element_type=f32)
        loaded += lax.dot_general(split[1], table, dims, preferred_element_type=f32)
        loaded += lax.dot_general(split[0], table, dims, preferred_element_type=f32)
        bent = jnp.tanh(loaded)
        tall = rep * K
        pair = iota((tall, width), 0) // K == iota((tall, width), 1) // paths
        for j in range(DATES // rep):
            strip = jnp.where(pair, bent[j * tall : (j + 1) * tall], 0.0).astype(bf16)
            basis[half, j * tall : (j + 1) * tall, j * width : (j + 1) * width] = strip

    def half_sums(half, hold=False):
        make_basis(half, hold)

        def block_sums(right):
            cuts = [slice(c * CHUNK, (c + 1) * CHUNK) for c in range(slots // CHUNK)]
            values = [jnp.dot(coef_v[cut], right, preferred_element_type=f32).astype(bf16) for cut in cuts]
            total = None
            for cut, value in zip(cuts, values):
                term = jnp.dot(onehot[:, cut], value, preferred_element_type=f32)
                total = term if total is None else total + term
            return total

        blocks = max(1, acc.shape[1] // COLS)
        if blocks == 1:
            acc[...] = block_sums(basis[half])
        else:

            def one(b, carry):
                side = pl.ds(pl.multiple_of(b * COLS, COLS), COLS)
                acc[:, side] = block_sums(basis[half, :, side])
                return carry

            lax.fori_loop(0, blocks, one, 0)
        for j in range(n):
            part[half, j] = acc[j * owned : (j + 1) * owned]

    def scatter(j, half, stage):
        return pltpu.make_async_remote_copy(
            src_ref=part.at[half, j],
            dst_ref=recv.at[half, me],
            send_sem=ss_sem.at[stage],
            recv_sem=sr_sem.at[half],
            device_id={"trade": j},
            device_id_type=MESH,
        )

    for role, got in ((is_early, near - 1), (is_even, near - 2), (is_odd, near - 2)):
        if role is is_early:

            @pl.when(role)
            def _():
                settle(fact, gr_sem.at[0], got)

        else:

            @pl.when(jnp.logical_and(role, is_final))
            def _():
                settle(fact, gr_sem.at[1], got - 2)

            @pl.when(jnp.logical_and(role, jnp.logical_not(is_final)))
            def _():
                settle(fact, gr_sem.at[1], got)

    @pl.when(is_hub)
    def _():
        pl.semaphore_wait(ready, 1)
        each(lambda i: relay(n - 1 - i).start(), 0, near, among=False)

    half_sums(mine, hold=True)

    @pl.when(is_late)
    def _():
        each(lambda j: scatter(j, mine, 0).start(), 0, n)
        each(lambda j: pass_coefs(j).start(), near, n)

    @pl.when(is_early)
    def _():
        each(lambda j: scatter(j, mine, 0).start(), 0, near)

    settle(fact, gr_sem.at[1 - mine], near)

    @pl.when(is_early)
    def _():
        each(lambda j: scatter(j, mine, 0).start(), near, n, among=False)


    @pl.when(is_early)
    def _():
        half_sums(1 - mine)
        each(lambda j: scatter(j, 1 - mine, 1).start(), 0, n)
        recv[1 - mine, me] = part[1 - mine, me]
        settle(recv_c, cr_sem, n - pool)

    @pl.when(is_late)
    def _():
        make_basis(1 - mine)

        @pl.when(is_final)
        def _():
            settle(fact, gr_sem.at[2], 2)
            make_basis(1)

        settle(recv_c, cr_sem, n - pool - 1)

    recv[mine, me] = part[mine, me]

    def pooled(first, half):
        rest = recv_c[first]
        for j in range(first + 1, n - pool):
            rest = rest + recv_c[j]
        pieces = []
        for i in range(3):
            pieces.append(rest.astype(bf16).astype(f32))
            rest = rest - pieces[i]
        stack = jnp.concatenate(pieces, axis=0).astype(bf16)
        thirds = jnp.dot(stack, basis[half], preferred_element_type=f32)
        return thirds[2 * owned :] + thirds[owned : 2 * owned] + thirds[:owned]

    recv[0, pool] = pooled(0, 0)
    held_back = iota((owned, DATES * paths), 1) % paths < 2 * rows
    recv[1, me] = recv[1, me] + jnp.where(held_back, pooled(n - 2 - pool, 1), 0.0)
    for j in range(pool + 1, n):
        recv[0, j] = jnp.zeros(recv.shape[2:], f32)

    row_at = iota((owned, 1), 0)
    limits = jnp.zeros((owned, 1), f32)
    for r in range(owned):
        limits = jnp.where(row_at == r, thr_s[r], limits)
    first = LAG * paths
    result = jnp.zeros(out.shape, f32)
    lane_date = iota((owned, width), 1) // paths
    column = iota(out.shape, 1)

    def shortfall(half):
        netted = recv[half, 0]
        for j in range(1, n):
            netted = netted + recv[half, j]
        margin = jnp.maximum(netted[:, : (DATES - LAG) * paths] - limits, 0.0)
        collateral = jnp.concatenate([held[half], margin], axis=1)
        return jnp.maximum(netted - collateral, 0.0)

    @pl.when(is_early)
    def _():
        settle(recv.at[0], sr_sem.at[0], pool - 1)

    @pl.when(is_late)
    def _():
        settle(recv.at[0], sr_sem.at[0], pool)

    short = shortfall(0)
    settle(recv.at[1], sr_sem.at[1], n - 1)
    short = short + shortfall(1)
    for j in range(DATES // rep):
        block = short[:, j * width : (j + 1) * width]
        for i in range(rep):
            own_date = jnp.where(lane_date == i, block, 0.0) if rep > 1 else block
            result = jnp.where(column == j * rep + i, jnp.sum(own_date, axis=1, keepdims=True), result)
    out[...] = result

    @pl.when(is_early)
    def _():
        settle(fact, gs_sem, near - 1)

    @pl.when(is_hub)
    def _():
        each(lambda j: settle(fact, gs_sem, near), near, n, among=False)

    @pl.when(is_even)
    def _():
        settle(fact, gs_sem, 1)

    @pl.when(is_odd)
    def _():
        settle(fact, gs_sem, n)
        settle(fact, gs_sem, n - 3)

    settle(recv.at[0], ss_sem.at[0], n - 1)

    @pl.when(is_early)
    def _():
        settle(recv.at[1], ss_sem.at[1], n - 1)

    @pl.when(is_late)
    def _():
        settle(part_c, cs_sem, n - 1)


def stay(x):
    return pltpu.with_memory_space_constraint(x, pltpu.MemorySpace.HBM)


def body(n, factors, loadings, trade_coef, basis_size, set_ids, live_count, netting_row, threshold, margin_start):
    rows = factors.shape[0]
    paths = n * rows
    half = paths // 2
    rep = max(1, LANES // half)
    slots = trade_coef.shape[0]
    sets = netting_row.shape[0]
    owned = threshold.shape[0]
    wide = DATES * half
    hbm = pl.BlockSpec(memory_space=pltpu.MemorySpace.HBM)
    total = pl.pallas_call(
        functools.partial(kernel, n),
        out_shape=jax.ShapeDtypeStruct((owned, DATES), f32),
        in_specs=[hbm] * 5 + [pl.BlockSpec(memory_space=pltpu.SMEM)] + [hbm] * 3,
        out_specs=pl.BlockSpec(memory_space=pltpu.VMEM),
        scratch_shapes=[
            pltpu.VMEM((n, rows, DATES * F), bf16),
            pltpu.VMEM((F, K), f32),
            pltpu.VMEM((slots, DATES * K), bf16),
            pltpu.VMEM((slots // LANES, LANES), jnp.int32),
            pltpu.VMEM((1, slots), jnp.int32),
            pltpu.VMEM((1, sets), jnp.int32),
            pltpu.SMEM((owned,), f32),
            pltpu.VMEM((owned, paths), f32),
            pltpu.VMEM((3, DATES * K, DATES * F), bf16),
            pltpu.VMEM((sets, slots), bf16),
            pltpu.VMEM((rep * half, DATES * F), f32),
            pltpu.VMEM((2, DATES * K, wide), bf16),
            pltpu.VMEM((2, owned, LAG * half), f32),
            pltpu.VMEM((sets, wide), f32),
            pltpu.VMEM((2, n, owned, wide), f32),
            pltpu.VMEM((2, n, owned, wide), f32),
            pltpu.VMEM((n, owned, DATES * K), f32),
            pltpu.VMEM((n // 2, owned, DATES * K), f32),
            pltpu.SemaphoreType.DMA((3,)),
            pltpu.SemaphoreType.DMA,
            pltpu.SemaphoreType.DMA((4,)),
            pltpu.SemaphoreType.DMA,
            pltpu.SemaphoreType.DMA((2,)),
            pltpu.SemaphoreType.DMA((2,)),
            pltpu.SemaphoreType.DMA,
            pltpu.SemaphoreType.DMA,
            pltpu.SemaphoreType.REGULAR,
        ],
        compiler_params=pltpu.CompilerParams(
            collective_id=0, has_side_effects=True, vmem_limit_bytes=48 * 2**20
        ),
    )(
        stay(factors),
        stay(loadings.T),
        stay(trade_coef),
        stay(basis_size.reshape(slots // LANES, LANES)),
        stay(set_ids.reshape(1, slots)),
        live_count,
        stay(netting_row.reshape(1, sets)),
        stay(threshold),
        stay(margin_start),
    )
    return total / paths


def solution(mesh):
    return jax.shard_map(
        functools.partial(body, mesh.shape["trade"]),
        mesh=mesh,
        in_specs=(
            P(("group", "trade"), None),
            P(),
            P(("group", "trade"), None),
            P(("group", "trade")),
            P(("group", "trade")),
            P(("group", "trade")),
            P("group"),
            P(("group", "trade")),
            P(("group", "trade"), None),
        ),
        out_specs=P(("group", "trade"), None),
        check_vma=False,
    )
```

```python
import functools

import jax
import jax.numpy as jnp
from jax import lax
from jax.experimental import pallas as pl
from jax.experimental.pallas import tpu as pltpu
from jax.sharding import PartitionSpec as P

F = 16
K = 32
DATES = 8
LAG = 2
LANES = 128
CHUNK = 256
COLS = 512
MESH = pl.DeviceIdType.MESH
f32 = jnp.float32
bf16 = jnp.bfloat16


def iota(shape, axis):
    return lax.broadcasted_iota(jnp.int32, shape, axis)


def kernel(
    n,
    factors,
    loadings,
    trade_coef,
    basis_size,
    set_ids,
    live_count,
    netting_row,
    threshold,
    margin_start,
    out,
    fact,
    load_v,
    coef_v,
    size_v,
    ids_v,
    nrow_v,
    thr_s,
    marg_v,
    split,
    onehot,
    spread,
    basis,
    held,
    acc,
    part,
    recv,
    part_c,
    recv_c,
    in_sem,
    gs_sem,
    gr_sem,
    pair_sem,
    ss_sem,
    sr_sem,
    cs_sem,
    cr_sem,
    ready,
):
    me = lax.axis_index("trade")
    rows = fact.shape[1]
    near = n // 2
    paths = near * rows
    rep = max(1, LANES // paths)
    width = rep * paths
    slots = coef_v.shape[0]
    owned = recv.shape[2]
    mine = lax.div(me, near)
    sets = n * owned

    quarter = n // 4
    hub = quarter + 1
    is_hub = me == hub
    is_late = me >= near
    slow = near + 1
    odd = lax.rem(me, 2) == 1
    even = jnp.logical_not(odd)
    is_odd = jnp.logical_and(is_late, odd)
    base = mine * near
    is_final = me >= n - 2
    pool = n - recv_c.shape[0]
    is_early = jnp.logical_not(is_late)

    def each(step, lo, hi, among=True):
        def at(i):
            step(jnp.where(i >= me, i + 1, i) if among else i)

        count = hi - lo - 1 if among else hi - lo
        if n <= LANES // 4:
            for i in range(lo, lo + count):
                at(i)
        else:
            lax.fori_loop(lo, lo + count, lambda i, c: (at(i), c)[1], 0)

    def local(src, dst, i):
        return pltpu.make_async_copy(src, dst, in_sem.at[i])

    def settle(ref, sem, count):
        rest = ref.at[pl.ds(0, count)]
        pltpu.make_async_copy(rest, rest, sem).wait()

    barrier = pltpu.get_barrier_semaphore()

    def greet(j):
        pl.semaphore_signal(barrier, inc=1, device_id={"trade": j}, device_id_type=MESH)

    def each_odd(step, start):
        def at(i):
            j = start + 1 + 2 * i

            @pl.when(j != me)
            def _():
                step(j)

        if n <= LANES // 4:
            for i in range(quarter - 1, -1, -1):
                at(i)
        else:
            lax.fori_loop(0, quarter, lambda i, c: (at(quarter - 1 - i), c)[1], 0)

    @pl.when(odd)
    def _():
        greet(me - 1)

    each_odd(greet, near)

    @pl.when(is_early)
    def _():
        each_odd(greet, 0)

    own = local(factors, fact.at[me], 0)
    limit_copy = local(threshold, thr_s, 1)
    pairs = (
        (loadings, load_v),
        (basis_size, size_v),
        (netting_row, nrow_v),
        (set_ids, ids_v),
        (margin_start, marg_v),
        (trade_coef, coef_v),
    )
    copies = [local(src, dst, 2) for src, dst in pairs]
    for copy in (own, *copies, limit_copy):
        copy.start()
    def gather(j):
        return pltpu.make_async_remote_copy(
            src_ref=fact.at[me],
            dst_ref=fact.at[me],
            send_sem=gs_sem,
            recv_sem=gr_sem.at[3],
            device_id={"trade": j},
            device_id_type=MESH,
        )

    def relay(j):
        return pltpu.make_async_remote_copy(
            src_ref=fact.at[pl.ds(0, near)],
            dst_ref=fact.at[pl.ds(0, near)],
            send_sem=gs_sem,
            recv_sem=gr_sem.at[0],
            device_id={"trade": j},
            device_id_type=MESH,
        )

    def to_partner():
        return pltpu.make_async_remote_copy(
            src_ref=factors,
            dst_ref=fact.at[me],
            send_sem=gs_sem,
            recv_sem=pair_sem,
            device_id={"trade": me + 1},
            device_id_type=MESH,
        )

    def pair(j):
        both = pl.ds(me - 1, 2)
        return pltpu.make_async_remote_copy(
            src_ref=fact.at[both],
            dst_ref=fact.at[both],
            send_sem=gs_sem,
            recv_sem=gr_sem.at[jnp.where(jnp.logical_and(me == slow, j >= n - 2), 2, mine)],
            device_id={"trade": j},
            device_id_type=MESH,
        )

    @pl.when(even)
    def _():
        pl.semaphore_wait(barrier, 1)
        to_partner().start()
        own.wait()

    @pl.when(odd)
    def _():
        own.wait()

        @pl.when(is_late)
        def _():
            pl.semaphore_wait(barrier, n - 1)

        @pl.when(is_early)
        def _():
            pl.semaphore_wait(barrier, near - 1)

        @pl.when(me == slow)
        def _():
            pl.semaphore_signal(ready, inc=1, device_id={"trade": hub}, device_id_type=MESH)

        gather(me - 1).start()
        settle(fact, pair_sem, 1)
        each_odd(lambda j: pair(j - 1).start(), base)
        each_odd(lambda j: pair(j).start(), base)

        @pl.when(is_late)
        def _():
            each(lambda j: pair(j).start(), 0, near, among=False)

    for copy in copies:
        copy.wait()
    limit_copy.wait()
    tiled = (iota((F, LANES), 1) % F == iota((F, LANES), 0)).astype(f32).astype(bf16)
    diag = iota((DATES * K, LANES), 0) // K == iota((DATES * K, LANES), 1) // F
    rest = load_v[...]
    for i in range(3):
        piece = rest.astype(bf16)
        rest = rest - piece.astype(f32)
        wide = lax.dot_general(piece, tiled, (((0,), (0,)), ((), ())), preferred_element_type=f32)
        wide = jnp.concatenate([wide] * DATES, axis=0)
        split[i] = jnp.where(diag, wide, 0.0).astype(bf16)
    basis[...] = jnp.zeros(basis.shape, bf16)

    found = nrow_v[...] == iota((sets, sets), 0)
    owner_set = jnp.sum(jnp.where(found, iota((sets, sets), 1), 0).astype(f32), axis=1, keepdims=True)
    owner_set = owner_set.astype(jnp.int32)
    for c in range(slots // CHUNK):
        cut = slice(c * CHUNK, (c + 1) * CHUNK)
        onehot[:, cut] = (ids_v[:, cut] == owner_set).astype(f32).astype(bf16)

    for half in range(2):
        for i in range(LAG):
            held[half, :, i * paths : (i + 1) * paths] = marg_v[:, half * paths : (half + 1) * paths]

    live_now = live_count[0]
    slot_index = iota(size_v.shape, 0) * LANES + iota(size_v.shape, 1)
    used = jnp.where(slot_index < live_now, size_v[...], 0).astype(f32)
    basis_index = (iota((LANES, LANES), 1) % K).astype(f32)
    for c in range(slots // LANES):
        limit = jnp.broadcast_to(used[c : c + 1], (LANES, LANES)).T
        keep = basis_index < limit
        cut = slice(c * LANES, (c + 1) * LANES)
        for h in range(0, DATES * K, LANES):
            side = slice(h, h + LANES)
            coef_v[cut, side] = jnp.where(keep, coef_v[cut, side].astype(f32), 0.0).astype(bf16)

    def pass_coefs(j):
        return pltpu.make_async_remote_copy(
            src_ref=part_c.at[j],
            dst_ref=recv_c.at[me - pool],
            send_sem=cs_sem,
            recv_sem=cr_sem,
            device_id={"trade": j},
            device_id_type=MESH,
        )

    @pl.when(is_late)
    def _():
        total = None
        for c in range(slots // CHUNK):
            cut = slice(c * CHUNK, (c + 1) * CHUNK)
            term = jnp.dot(onehot[:, cut], coef_v[cut], preferred_element_type=f32)
            total = term if total is None else total + term
        for j in range(n):
            part_c[j] = total[j * owned : (j + 1) * owned]

        @pl.when(even)
        def _():
            settle(fact, gr_sem.at[3], 1)

        each(lambda j: pass_coefs(j).start(), 0, near, among=False)
        recv_c[me - pool] = part_c[me]

    def make_basis(half, hold=False):
        for j in range(near):

            def fill(j=j):
                block = fact[half * near + j].astype(f32)
                for i in range(rep):
                    at = i * paths + j * rows
                    spread[at : at + rows] = block

            if hold and j < 2:
                pl.when(jnp.logical_not(is_final))(fill)

                @pl.when(is_final)
                def _():
                    for i in range(rep):
                        at = i * paths + j * rows
                        spread[at : at + rows] = jnp.zeros((rows, spread.shape[1]), f32)

            else:
                fill()
        table = spread[...].astype(bf16)
        dims = (((1,), (1,)), ((), ()))
        loaded = lax.dot_general(split[2], table, dims, preferred_element_type=f32)
        loaded += lax.dot_general(split[1], table, dims, preferred_element_type=f32)
        loaded += lax.dot_general(split[0], table, dims, preferred_element_type=f32)
        bent = jnp.tanh(loaded)
        tall = rep * K
        pair = iota((tall, width), 0) // K == iota((tall, width), 1) // paths
        for j in range(DATES // rep):
            strip = jnp.where(pair, bent[j * tall : (j + 1) * tall], 0.0).astype(bf16)
            basis[half, j * tall : (j + 1) * tall, j * width : (j + 1) * width] = strip

    def half_sums(half, hold=False):
        make_basis(half, hold)

        def block_sums(right):
            cuts = [slice(c * CHUNK, (c + 1) * CHUNK) for c in range(slots // CHUNK)]
            values = [jnp.dot(coef_v[cut], right, preferred_element_type=f32).astype(bf16) for cut in cuts]
            total = None
            for cut, value in zip(cuts, values):
                term = jnp.dot(onehot[:, cut], value, preferred_element_type=f32)
                total = term if total is None else total + term
            return total

        blocks = max(1, acc.shape[1] // COLS)
        if blocks == 1:
            acc[...] = block_sums(basis[half])
        else:

            def one(b, carry):
                side = pl.ds(pl.multiple_of(b * COLS, COLS), COLS)
                acc[:, side] = block_sums(basis[half, :, side])
                return carry

            lax.fori_loop(0, blocks, one, 0)
        for j in range(n):
            part[half, j] = acc[j * owned : (j + 1) * owned]

    def scatter(j, half, stage):
        return pltpu.make_async_remote_copy(
            src_ref=part.at[half, j],
            dst_ref=recv.at[half, me],
            send_sem=ss_sem.at[stage],
            recv_sem=sr_sem.at[half],
            device_id={"trade": j},
            device_id_type=MESH,
        )

    @pl.when(jnp.logical_and(is_early, even))
    def _():
        settle(fact, gr_sem.at[3], 1)

    @pl.when(is_final)
    def _():
        settle(fact, gr_sem.at[1], near - 4)

    @pl.when(jnp.logical_not(is_final))
    def _():
        settle(fact, gr_sem.at[mine], near - 2)

    @pl.when(is_hub)
    def _():
        pl.semaphore_wait(ready, 1)
        each(lambda i: relay(n - 1 - i).start(), 0, near, among=False)

    half_sums(mine, hold=True)

    @pl.when(is_late)
    def _():
        each(lambda j: scatter(j, mine, 0).start(), 0, n)
        each(lambda j: pass_coefs(j).start(), near, n)

    @pl.when(is_early)
    def _():
        each(lambda j: scatter(j, mine, 0).start(), 0, near)

    settle(fact, gr_sem.at[1 - mine], near)

    @pl.when(is_early)
    def _():
        each(lambda j: scatter(j, mine, 0).start(), near, n, among=False)


    @pl.when(is_early)
    def _():
        half_sums(1 - mine)
        each(lambda j: scatter(j, 1 - mine, 1).start(), 0, n)
        recv[1 - mine, me] = part[1 - mine, me]
        settle(recv_c, cr_sem, n - pool)

    @pl.when(is_late)
    def _():
        make_basis(1 - mine)

        @pl.when(is_final)
        def _():
            settle(fact, gr_sem.at[2], 2)
            make_basis(1)

        settle(recv_c, cr_sem, n - pool - 1)

    recv[mine, me] = part[mine, me]

    def pooled(first, half):
        rest = recv_c[first]
        for j in range(first + 1, n - pool):
            rest = rest + recv_c[j]
        pieces = []
        for i in range(3):
            pieces.append(rest.astype(bf16).astype(f32))
            rest = rest - pieces[i]
        stack = jnp.concatenate(pieces, axis=0).astype(bf16)
        thirds = jnp.dot(stack, basis[half], preferred_element_type=f32)
        return thirds[2 * owned :] + thirds[owned : 2 * owned] + thirds[:owned]

    recv[0, pool] = pooled(0, 0)
    held_back = iota((owned, DATES * paths), 1) % paths < 2 * rows
    recv[1, me] = recv[1, me] + jnp.where(held_back, pooled(n - 2 - pool, 1), 0.0)
    for j in range(pool + 1, n):
        recv[0, j] = jnp.zeros(recv.shape[2:], f32)

    row_at = iota((owned, 1), 0)
    limits = jnp.zeros((owned, 1), f32)
    for r in range(owned):
        limits = jnp.where(row_at == r, thr_s[r], limits)
    first = LAG * paths
    result = jnp.zeros(out.shape, f32)
    lane_date = iota((owned, width), 1) // paths
    column = iota(out.shape, 1)

    def shortfall(half):
        netted = recv[half, 0]
        for j in range(1, n):
            netted = netted + recv[half, j]
        margin = jnp.maximum(netted[:, : (DATES - LAG) * paths] - limits, 0.0)
        collateral = jnp.concatenate([held[half], margin], axis=1)
        return jnp.maximum(netted - collateral, 0.0)

    @pl.when(is_early)
    def _():
        settle(recv.at[0], sr_sem.at[0], pool - 1)

    @pl.when(is_late)
    def _():
        settle(recv.at[0], sr_sem.at[0], pool)

    short = shortfall(0)
    settle(recv.at[1], sr_sem.at[1], n - 1)
    short = short + shortfall(1)
    for j in range(DATES // rep):
        block = short[:, j * width : (j + 1) * width]
        for i in range(rep):
            own_date = jnp.where(lane_date == i, block, 0.0) if rep > 1 else block
            result = jnp.where(column == j * rep + i, jnp.sum(own_date, axis=1, keepdims=True), result)
    out[...] = result

    @pl.when(jnp.logical_and(is_early, odd))
    def _():
        settle(fact, gs_sem, near)
        settle(fact, gs_sem, near - 3)

    @pl.when(is_hub)
    def _():
        each(lambda j: settle(fact, gs_sem, near), near, n, among=False)

    @pl.when(even)
    def _():
        settle(fact, gs_sem, 1)

    @pl.when(is_odd)
    def _():
        settle(fact, gs_sem, n)
        settle(fact, gs_sem, n - 3)

    settle(recv.at[0], ss_sem.at[0], n - 1)

    @pl.when(is_early)
    def _():
        settle(recv.at[1], ss_sem.at[1], n - 1)

    @pl.when(is_late)
    def _():
        settle(part_c, cs_sem, n - 1)


def stay(x):
    return pltpu.with_memory_space_constraint(x, pltpu.MemorySpace.HBM)


def body(n, factors, loadings, trade_coef, basis_size, set_ids, live_count, netting_row, threshold, margin_start):
    rows = factors.shape[0]
    paths = n * rows
    half = paths // 2
    rep = max(1, LANES // half)
    slots = trade_coef.shape[0]
    sets = netting_row.shape[0]
    owned = threshold.shape[0]
    wide = DATES * half
    hbm = pl.BlockSpec(memory_space=pltpu.MemorySpace.HBM)
    total = pl.pallas_call(
        functools.partial(kernel, n),
        out_shape=jax.ShapeDtypeStruct((owned, DATES), f32),
        in_specs=[hbm] * 5 + [pl.BlockSpec(memory_space=pltpu.SMEM)] + [hbm] * 3,
        out_specs=pl.BlockSpec(memory_space=pltpu.VMEM),
        scratch_shapes=[
            pltpu.VMEM((n, rows, DATES * F), bf16),
            pltpu.VMEM((F, K), f32),
            pltpu.VMEM((slots, DATES * K), bf16),
            pltpu.VMEM((slots // LANES, LANES), jnp.int32),
            pltpu.VMEM((1, slots), jnp.int32),
            pltpu.VMEM((1, sets), jnp.int32),
            pltpu.SMEM((owned,), f32),
            pltpu.VMEM((owned, paths), f32),
            pltpu.VMEM((3, DATES * K, DATES * F), bf16),
            pltpu.VMEM((sets, slots), bf16),
            pltpu.VMEM((rep * half, DATES * F), f32),
            pltpu.VMEM((2, DATES * K, wide), bf16),
            pltpu.VMEM((2, owned, LAG * half), f32),
            pltpu.VMEM((sets, wide), f32),
            pltpu.VMEM((2, n, owned, wide), f32),
            pltpu.VMEM((2, n, owned, wide), f32),
            pltpu.VMEM((n, owned, DATES * K), f32),
            pltpu.VMEM((n // 2, owned, DATES * K), f32),
            pltpu.SemaphoreType.DMA((3,)),
            pltpu.SemaphoreType.DMA,
            pltpu.SemaphoreType.DMA((4,)),
            pltpu.SemaphoreType.DMA,
            pltpu.SemaphoreType.DMA((2,)),
            pltpu.SemaphoreType.DMA((2,)),
            pltpu.SemaphoreType.DMA,
            pltpu.SemaphoreType.DMA,
            pltpu.SemaphoreType.REGULAR,
        ],
        compiler_params=pltpu.CompilerParams(
            collective_id=0, has_side_effects=True, vmem_limit_bytes=48 * 2**20
        ),
    )(
        stay(factors),
        stay(loadings.T),
        stay(trade_coef),
        stay(basis_size.reshape(slots // LANES, LANES)),
        stay(set_ids.reshape(1, slots)),
        live_count,
        stay(netting_row.reshape(1, sets)),
        stay(threshold),
        stay(margin_start),
    )
    return total / paths


def solution(mesh):
    return jax.shard_map(
        functools.partial(body, mesh.shape["trade"]),
        mesh=mesh,
        in_specs=(
            P(("group", "trade"), None),
            P(),
            P(("group", "trade"), None),
            P(("group", "trade")),
            P(("group", "trade")),
            P(("group", "trade")),
            P("group"),
            P(("group", "trade")),
            P(("group", "trade"), None),
        ),
        out_specs=P(("group", "trade"), None),
        check_vma=False,
    )
```

```python
import functools

import jax
import jax.numpy as jnp
from jax import lax
from jax.experimental import pallas as pl
from jax.experimental.pallas import tpu as pltpu
from jax.sharding import PartitionSpec as P

F = 16
K = 32
DATES = 8
LAG = 2
LANES = 128
CHUNK = 128
COLS = 512
MESH = pl.DeviceIdType.MESH
f32 = jnp.float32
bf16 = jnp.bfloat16


def iota(shape, axis):
    return lax.broadcasted_iota(jnp.int32, shape, axis)


def kernel(
    n,
    factors,
    loadings,
    trade_coef,
    basis_size,
    set_ids,
    live_count,
    netting_row,
    threshold,
    margin_start,
    out,
    fact,
    load_v,
    coef_v,
    size_v,
    ids_v,
    nrow_v,
    thr_s,
    marg_v,
    split,
    onehot,
    spread,
    basis,
    held,
    acc,
    part,
    recv,
    part_c,
    recv_c,
    in_sem,
    gs_sem,
    gr_sem,
    pair_sem,
    ss_sem,
    sr_sem,
    cs_sem,
    cr_sem,
    ready,
):
    me = lax.axis_index("trade")
    rows = fact.shape[1]
    near = n // 2
    paths = near * rows
    rep = max(1, LANES // paths)
    width = rep * paths
    slots = coef_v.shape[0]
    owned = recv.shape[2]
    mine = lax.div(me, near)
    sets = n * owned

    quarter = n // 4
    hub = quarter + 1
    is_hub = me == hub
    is_late = me >= near
    slow = near + 1
    odd = lax.rem(me, 2) == 1
    even = jnp.logical_not(odd)
    is_odd = jnp.logical_and(is_late, odd)
    base = mine * near
    is_final = me >= n - 2
    pool = n - recv_c.shape[0]
    is_early = jnp.logical_not(is_late)

    def each(step, lo, hi, among=True):
        def at(i):
            step(jnp.where(i >= me, i + 1, i) if among else i)

        count = hi - lo - 1 if among else hi - lo
        if n <= LANES // 4:
            for i in range(lo, lo + count):
                at(i)
        else:
            lax.fori_loop(lo, lo + count, lambda i, c: (at(i), c)[1], 0)

    def local(src, dst, i):
        return pltpu.make_async_copy(src, dst, in_sem.at[i])

    def settle(ref, sem, count):
        rest = ref.at[pl.ds(0, count)]
        pltpu.make_async_copy(rest, rest, sem).wait()

    barrier = pltpu.get_barrier_semaphore()

    def greet(j):
        pl.semaphore_signal(barrier, inc=1, device_id={"trade": j}, device_id_type=MESH)

    def each_odd(step, start):
        def at(i):
            j = start + 1 + 2 * i

            @pl.when(j != me)
            def _():
                step(j)

        if n <= LANES // 4:
            for i in range(quarter - 1, -1, -1):
                at(i)
        else:
            lax.fori_loop(0, quarter, lambda i, c: (at(quarter - 1 - i), c)[1], 0)

    @pl.when(odd)
    def _():
        greet(me - 1)

    each_odd(greet, near)

    @pl.when(is_early)
    def _():
        each_odd(greet, 0)

    own = local(factors, fact.at[me], 0)
    limit_copy = local(threshold, thr_s, 1)
    pairs = (
        (loadings, load_v),
        (basis_size, size_v),
        (netting_row, nrow_v),
        (set_ids, ids_v),
        (margin_start, marg_v),
        (trade_coef, coef_v),
    )
    copies = [local(src, dst, 2) for src, dst in pairs]
    for copy in (own, *copies, limit_copy):
        copy.start()
    def gather(j):
        return pltpu.make_async_remote_copy(
            src_ref=fact.at[me],
            dst_ref=fact.at[me],
            send_sem=gs_sem,
            recv_sem=gr_sem.at[3],
            device_id={"trade": j},
            device_id_type=MESH,
        )

    def relay(j):
        return pltpu.make_async_remote_copy(
            src_ref=fact.at[pl.ds(0, near)],
            dst_ref=fact.at[pl.ds(0, near)],
            send_sem=gs_sem,
            recv_sem=gr_sem.at[0],
            device_id={"trade": j},
            device_id_type=MESH,
        )

    def to_partner():
        return pltpu.make_async_remote_copy(
            src_ref=factors,
            dst_ref=fact.at[me],
            send_sem=gs_sem,
            recv_sem=pair_sem,
            device_id={"trade": me + 1},
            device_id_type=MESH,
        )

    def pair(j):
        both = pl.ds(me - 1, 2)
        return pltpu.make_async_remote_copy(
            src_ref=fact.at[both],
            dst_ref=fact.at[both],
            send_sem=gs_sem,
            recv_sem=gr_sem.at[jnp.where(jnp.logical_and(me == slow, j >= n - 2), 2, mine)],
            device_id={"trade": j},
            device_id_type=MESH,
        )

    @pl.when(even)
    def _():
        pl.semaphore_wait(barrier, 1)
        to_partner().start()
        own.wait()

    @pl.when(odd)
    def _():
        own.wait()

        @pl.when(is_late)
        def _():
            pl.semaphore_wait(barrier, n - 1)

        @pl.when(is_early)
        def _():
            pl.semaphore_wait(barrier, near - 1)

        @pl.when(me == slow)
        def _():
            pl.semaphore_signal(ready, inc=1, device_id={"trade": hub}, device_id_type=MESH)

        gather(me - 1).start()
        settle(fact, pair_sem, 1)
        each_odd(lambda j: pair(j - 1).start(), base)
        each_odd(lambda j: pair(j).start(), base)

        @pl.when(is_late)
        def _():
            each(lambda j: pair(j).start(), 0, near, among=False)

    for copy in copies:
        copy.wait()
    limit_copy.wait()
    tiled = (iota((F, LANES), 1) % F == iota((F, LANES), 0)).astype(f32).astype(bf16)
    diag = iota((DATES * K, LANES), 0) // K == iota((DATES * K, LANES), 1) // F
    rest = load_v[...]
    for i in range(3):
        piece = rest.astype(bf16)
        rest = rest - piece.astype(f32)
        wide = lax.dot_general(piece, tiled, (((0,), (0,)), ((), ())), preferred_element_type=f32)
        wide = jnp.concatenate([wide] * DATES, axis=0)
        split[i] = jnp.where(diag, wide, 0.0).astype(bf16)
    basis[...] = jnp.zeros(basis.shape, bf16)

    found = nrow_v[...] == iota((sets, sets), 0)
    owner_set = jnp.sum(jnp.where(found, iota((sets, sets), 1), 0).astype(f32), axis=1, keepdims=True)
    owner_set = owner_set.astype(jnp.int32)
    for c in range(slots // CHUNK):
        cut = slice(c * CHUNK, (c + 1) * CHUNK)
        onehot[:, cut] = (ids_v[:, cut] == owner_set).astype(f32).astype(bf16)

    for half in range(2):
        for i in range(LAG):
            held[half, :, i * paths : (i + 1) * paths] = marg_v[:, half * paths : (half + 1) * paths]

    live_now = live_count[0]
    slot_index = iota(size_v.shape, 0) * LANES + iota(size_v.shape, 1)
    used = jnp.where(slot_index < live_now, size_v[...], 0).astype(f32)
    basis_index = (iota((LANES, LANES), 1) % K).astype(f32)
    for c in range(slots // LANES):
        limit = jnp.broadcast_to(used[c : c + 1], (LANES, LANES)).T
        keep = basis_index < limit
        cut = slice(c * LANES, (c + 1) * LANES)
        for h in range(0, DATES * K, LANES):
            side = slice(h, h + LANES)
            coef_v[cut, side] = jnp.where(keep, coef_v[cut, side].astype(f32), 0.0).astype(bf16)

    def pass_coefs(j):
        return pltpu.make_async_remote_copy(
            src_ref=part_c.at[j],
            dst_ref=recv_c.at[me - pool],
            send_sem=cs_sem,
            recv_sem=cr_sem,
            device_id={"trade": j},
            device_id_type=MESH,
        )

    @pl.when(is_late)
    def _():
        total = None
        for c in range(slots // CHUNK):
            cut = slice(c * CHUNK, (c + 1) * CHUNK)
            term = jnp.dot(onehot[:, cut], coef_v[cut], preferred_element_type=f32)
            total = term if total is None else total + term
        for j in range(n):
            part_c[j] = total[j * owned : (j + 1) * owned]

        @pl.when(even)
        def _():
            settle(fact, gr_sem.at[3], 1)

        each(lambda j: pass_coefs(j).start(), 0, near, among=False)
        recv_c[me - pool] = part_c[me]

    def make_basis(half, hold=False):
        for j in range(near):

            def fill(j=j):
                block = fact[half * near + j].astype(f32)
                for i in range(rep):
                    at = i * paths + j * rows
                    spread[at : at + rows] = block

            if hold and j < 2:
                pl.when(jnp.logical_not(is_final))(fill)

                @pl.when(is_final)
                def _():
                    for i in range(rep):
                        at = i * paths + j * rows
                        spread[at : at + rows] = jnp.zeros((rows, spread.shape[1]), f32)

            else:
                fill()
        table = spread[...].astype(bf16)
        dims = (((1,), (1,)), ((), ()))
        loaded = lax.dot_general(split[2], table, dims, preferred_element_type=f32)
        loaded += lax.dot_general(split[1], table, dims, preferred_element_type=f32)
        loaded += lax.dot_general(split[0], table, dims, preferred_element_type=f32)
        bent = jnp.tanh(loaded)
        tall = rep * K
        pair = iota((tall, width), 0) // K == iota((tall, width), 1) // paths
        for j in range(DATES // rep):
            strip = jnp.where(pair, bent[j * tall : (j + 1) * tall], 0.0).astype(bf16)
            basis[half, j * tall : (j + 1) * tall, j * width : (j + 1) * width] = strip

    def half_sums(half, hold=False):
        make_basis(half, hold)

        def block_sums(right):
            cuts = [slice(c * CHUNK, (c + 1) * CHUNK) for c in range(slots // CHUNK)]
            values = [jnp.dot(coef_v[cut], right, preferred_element_type=f32).astype(bf16) for cut in cuts]
            total = None
            for cut, value in zip(cuts, values):
                term = jnp.dot(onehot[:, cut], value, preferred_element_type=f32)
                total = term if total is None else total + term
            return total

        blocks = max(1, acc.shape[1] // COLS)
        if blocks == 1:
            acc[...] = block_sums(basis[half])
        else:

            def one(b, carry):
                side = pl.ds(pl.multiple_of(b * COLS, COLS), COLS)
                acc[:, side] = block_sums(basis[half, :, side])
                return carry

            lax.fori_loop(0, blocks, one, 0)
        for j in range(n):
            part[half, j] = acc[j * owned : (j + 1) * owned]

    def scatter(j, half, stage):
        return pltpu.make_async_remote_copy(
            src_ref=part.at[half, j],
            dst_ref=recv.at[half, me],
            send_sem=ss_sem.at[stage],
            recv_sem=sr_sem.at[half],
            device_id={"trade": j},
            device_id_type=MESH,
        )

    @pl.when(jnp.logical_and(is_early, even))
    def _():
        settle(fact, gr_sem.at[3], 1)

    @pl.when(is_final)
    def _():
        settle(fact, gr_sem.at[1], near - 4)

    @pl.when(jnp.logical_not(is_final))
    def _():
        settle(fact, gr_sem.at[mine], near - 2)

    @pl.when(is_hub)
    def _():
        pl.semaphore_wait(ready, 1)
        each(lambda i: relay(n - 1 - i).start(), 0, near, among=False)

    half_sums(mine, hold=True)

    @pl.when(is_late)
    def _():
        each(lambda j: scatter(j, mine, 0).start(), 0, n)
        each(lambda j: pass_coefs(j).start(), near, n)

    @pl.when(is_early)
    def _():
        each(lambda j: scatter(j, mine, 0).start(), 0, near)

    settle(fact, gr_sem.at[1 - mine], near)

    @pl.when(is_early)
    def _():
        each(lambda j: scatter(j, mine, 0).start(), near, n, among=False)


    @pl.when(is_early)
    def _():
        half_sums(1 - mine)
        each(lambda j: scatter(j, 1 - mine, 1).start(), 0, n)
        recv[1 - mine, me] = part[1 - mine, me]
        settle(recv_c, cr_sem, n - pool)

    @pl.when(is_late)
    def _():
        make_basis(1 - mine)

        @pl.when(is_final)
        def _():
            settle(fact, gr_sem.at[2], 2)
            make_basis(1)

        settle(recv_c, cr_sem, n - pool - 1)

    recv[mine, me] = part[mine, me]

    def pooled(first, half):
        rest = recv_c[first]
        for j in range(first + 1, n - pool):
            rest = rest + recv_c[j]
        pieces = []
        for i in range(3):
            pieces.append(rest.astype(bf16).astype(f32))
            rest = rest - pieces[i]
        stack = jnp.concatenate(pieces, axis=0).astype(bf16)
        thirds = jnp.dot(stack, basis[half], preferred_element_type=f32)
        return thirds[2 * owned :] + thirds[owned : 2 * owned] + thirds[:owned]

    recv[0, pool] = pooled(0, 0)
    held_back = iota((owned, DATES * paths), 1) % paths < 2 * rows
    recv[1, me] = recv[1, me] + jnp.where(held_back, pooled(n - 2 - pool, 1), 0.0)
    for j in range(pool + 1, n):
        recv[0, j] = jnp.zeros(recv.shape[2:], f32)

    row_at = iota((owned, 1), 0)
    limits = jnp.zeros((owned, 1), f32)
    for r in range(owned):
        limits = jnp.where(row_at == r, thr_s[r], limits)
    first = LAG * paths
    result = jnp.zeros(out.shape, f32)
    lane_date = iota((owned, width), 1) // paths
    column = iota(out.shape, 1)

    def shortfall(half):
        netted = recv[half, 0]
        for j in range(1, n):
            netted = netted + recv[half, j]
        margin = jnp.maximum(netted[:, : (DATES - LAG) * paths] - limits, 0.0)
        collateral = jnp.concatenate([held[half], margin], axis=1)
        return jnp.maximum(netted - collateral, 0.0)

    @pl.when(is_early)
    def _():
        settle(recv.at[0], sr_sem.at[0], pool - 1)

    @pl.when(is_late)
    def _():
        settle(recv.at[0], sr_sem.at[0], pool)

    short = shortfall(0)
    settle(recv.at[1], sr_sem.at[1], n - 1)
    short = short + shortfall(1)
    for j in range(DATES // rep):
        block = short[:, j * width : (j + 1) * width]
        for i in range(rep):
            own_date = jnp.where(lane_date == i, block, 0.0) if rep > 1 else block
            result = jnp.where(column == j * rep + i, jnp.sum(own_date, axis=1, keepdims=True), result)
    out[...] = result

    @pl.when(jnp.logical_and(is_early, odd))
    def _():
        settle(fact, gs_sem, near)
        settle(fact, gs_sem, near - 3)

    @pl.when(is_hub)
    def _():
        each(lambda j: settle(fact, gs_sem, near), near, n, among=False)

    @pl.when(even)
    def _():
        settle(fact, gs_sem, 1)

    @pl.when(is_odd)
    def _():
        settle(fact, gs_sem, n)
        settle(fact, gs_sem, n - 3)

    settle(recv.at[0], ss_sem.at[0], n - 1)

    @pl.when(is_early)
    def _():
        settle(recv.at[1], ss_sem.at[1], n - 1)

    @pl.when(is_late)
    def _():
        settle(part_c, cs_sem, n - 1)


def stay(x):
    return pltpu.with_memory_space_constraint(x, pltpu.MemorySpace.HBM)


def body(n, factors, loadings, trade_coef, basis_size, set_ids, live_count, netting_row, threshold, margin_start):
    rows = factors.shape[0]
    paths = n * rows
    half = paths // 2
    rep = max(1, LANES // half)
    slots = trade_coef.shape[0]
    sets = netting_row.shape[0]
    owned = threshold.shape[0]
    wide = DATES * half
    hbm = pl.BlockSpec(memory_space=pltpu.MemorySpace.HBM)
    total = pl.pallas_call(
        functools.partial(kernel, n),
        out_shape=jax.ShapeDtypeStruct((owned, DATES), f32),
        in_specs=[hbm] * 5 + [pl.BlockSpec(memory_space=pltpu.SMEM)] + [hbm] * 3,
        out_specs=pl.BlockSpec(memory_space=pltpu.VMEM),
        scratch_shapes=[
            pltpu.VMEM((n, rows, DATES * F), bf16),
            pltpu.VMEM((F, K), f32),
            pltpu.VMEM((slots, DATES * K), bf16),
            pltpu.VMEM((slots // LANES, LANES), jnp.int32),
            pltpu.VMEM((1, slots), jnp.int32),
            pltpu.VMEM((1, sets), jnp.int32),
            pltpu.SMEM((owned,), f32),
            pltpu.VMEM((owned, paths), f32),
            pltpu.VMEM((3, DATES * K, DATES * F), bf16),
            pltpu.VMEM((sets, slots), bf16),
            pltpu.VMEM((rep * half, DATES * F), f32),
            pltpu.VMEM((2, DATES * K, wide), bf16),
            pltpu.VMEM((2, owned, LAG * half), f32),
            pltpu.VMEM((sets, wide), f32),
            pltpu.VMEM((2, n, owned, wide), f32),
            pltpu.VMEM((2, n, owned, wide), f32),
            pltpu.VMEM((n, owned, DATES * K), f32),
            pltpu.VMEM((n // 2, owned, DATES * K), f32),
            pltpu.SemaphoreType.DMA((3,)),
            pltpu.SemaphoreType.DMA,
            pltpu.SemaphoreType.DMA((4,)),
            pltpu.SemaphoreType.DMA,
            pltpu.SemaphoreType.DMA((2,)),
            pltpu.SemaphoreType.DMA((2,)),
            pltpu.SemaphoreType.DMA,
            pltpu.SemaphoreType.DMA,
            pltpu.SemaphoreType.REGULAR,
        ],
        compiler_params=pltpu.CompilerParams(
            collective_id=0, has_side_effects=True, vmem_limit_bytes=48 * 2**20
        ),
    )(
        stay(factors),
        stay(loadings.T),
        stay(trade_coef),
        stay(basis_size.reshape(slots // LANES, LANES)),
        stay(set_ids.reshape(1, slots)),
        live_count,
        stay(netting_row.reshape(1, sets)),
        stay(threshold),
        stay(margin_start),
    )
    return total / paths


def solution(mesh):
    return jax.shard_map(
        functools.partial(body, mesh.shape["trade"]),
        mesh=mesh,
        in_specs=(
            P(("group", "trade"), None),
            P(),
            P(("group", "trade"), None),
            P(("group", "trade")),
            P(("group", "trade")),
            P(("group", "trade")),
            P("group"),
            P(("group", "trade")),
            P(("group", "trade"), None),
        ),
        out_specs=P(("group", "trade"), None),
        check_vma=False,
    )
```

```python
import functools

import jax
import jax.numpy as jnp
from jax import lax
from jax.experimental import pallas as pl
from jax.experimental.pallas import tpu as pltpu
from jax.sharding import PartitionSpec as P

F = 16
K = 32
DATES = 8
LAG = 2
LANES = 128
CHUNK = 256
COLS = 512
MESH = pl.DeviceIdType.MESH
f32 = jnp.float32
bf16 = jnp.bfloat16


def iota(shape, axis):
    return lax.broadcasted_iota(jnp.int32, shape, axis)


def kernel(
    n,
    factors,
    loadings,
    trade_coef,
    basis_size,
    set_ids,
    live_count,
    netting_row,
    threshold,
    margin_start,
    out,
    fact,
    load_v,
    coef_v,
    size_v,
    ids_v,
    nrow_v,
    thr_s,
    marg_v,
    split,
    onehot,
    spread,
    basis,
    held,
    acc,
    part,
    recv,
    part_c,
    recv_c,
    in_sem,
    gs_sem,
    gr_sem,
    pair_sem,
    ss_sem,
    sr_sem,
    cs_sem,
    cr_sem,
    ready,
):
    me = lax.axis_index("trade")
    rows = fact.shape[1]
    near = n // 2
    paths = near * rows
    rep = max(1, LANES // paths)
    width = rep * paths
    slots = coef_v.shape[0]
    owned = recv.shape[2]
    mine = lax.div(me, near)
    sets = n * owned

    quarter = n // 4
    hub = quarter + 1
    is_hub = me == hub
    is_late = me >= near
    slow = near + 1
    helper = near + 3
    odd = lax.rem(me, 2) == 1
    even = jnp.logical_not(odd)
    is_odd = jnp.logical_and(is_late, odd)
    base = mine * near
    is_final = me >= n - 2
    pool = n - recv_c.shape[0]
    is_early = jnp.logical_not(is_late)

    def each(step, lo, hi, among=True):
        def at(i):
            step(jnp.where(i >= me, i + 1, i) if among else i)

        count = hi - lo - 1 if among else hi - lo
        if n <= LANES // 4:
            for i in range(lo, lo + count):
                at(i)
        else:
            lax.fori_loop(lo, lo + count, lambda i, c: (at(i), c)[1], 0)

    def local(src, dst, i):
        return pltpu.make_async_copy(src, dst, in_sem.at[i])

    def settle(ref, sem, count):
        rest = ref.at[pl.ds(0, count)]
        pltpu.make_async_copy(rest, rest, sem).wait()

    barrier = pltpu.get_barrier_semaphore()

    def greet(j):
        pl.semaphore_signal(barrier, inc=1, device_id={"trade": j}, device_id_type=MESH)

    def each_odd(step, start):
        def at(i):
            j = start + 1 + 2 * i

            @pl.when(j != me)
            def _():
                step(j)

        if n <= LANES // 4:
            for i in range(quarter - 1, -1, -1):
                at(i)
        else:
            lax.fori_loop(0, quarter, lambda i, c: (at(quarter - 1 - i), c)[1], 0)

    @pl.when(odd)
    def _():
        greet(me - 1)

    def greet_late(j):
        @pl.when(jnp.logical_not(jnp.logical_and(is_final, j == slow)))
        def _():
            greet(j)

    each_odd(greet_late, near)

    @pl.when(is_early)
    def _():
        each_odd(greet, 0)

    own = local(factors, fact.at[me], 0)
    limit_copy = local(threshold, thr_s, 1)
    pairs = (
        (loadings, load_v),
        (basis_size, size_v),
        (netting_row, nrow_v),
        (set_ids, ids_v),
        (margin_start, marg_v),
        (trade_coef, coef_v),
    )
    copies = [local(src, dst, 2) for src, dst in pairs]
    for copy in (own, *copies, limit_copy):
        copy.start()
    def gather(j):
        return pltpu.make_async_remote_copy(
            src_ref=fact.at[me],
            dst_ref=fact.at[me],
            send_sem=gs_sem,
            recv_sem=gr_sem.at[3],
            device_id={"trade": j},
            device_id_type=MESH,
        )

    def relay(j):
        return pltpu.make_async_remote_copy(
            src_ref=fact.at[pl.ds(0, near)],
            dst_ref=fact.at[pl.ds(0, near)],
            send_sem=gs_sem,
            recv_sem=gr_sem.at[0],
            device_id={"trade": j},
            device_id_type=MESH,
        )

    def to_partner():
        return pltpu.make_async_remote_copy(
            src_ref=factors,
            dst_ref=fact.at[me],
            send_sem=gs_sem,
            recv_sem=pair_sem,
            device_id={"trade": me + 1},
            device_id_type=MESH,
        )

    def pair(j):
        both = pl.ds(me - 1, 2)
        return pltpu.make_async_remote_copy(
            src_ref=fact.at[both],
            dst_ref=fact.at[both],
            send_sem=gs_sem,
            recv_sem=gr_sem.at[mine],
            device_id={"trade": j},
            device_id_type=MESH,
        )

    @pl.when(even)
    def _():
        pl.semaphore_wait(barrier, 1)
        to_partner().start()
        own.wait()

    @pl.when(odd)
    def _():
        own.wait()

        @pl.when(jnp.logical_and(is_late, me != slow))
        def _():
            pl.semaphore_wait(barrier, n - 1)

        @pl.when(me == slow)
        def _():
            pl.semaphore_wait(barrier, n - 3)

        @pl.when(is_early)
        def _():
            pl.semaphore_wait(barrier, near - 1)

        @pl.when(me == helper)
        def _():
            pl.semaphore_signal(ready, inc=1, device_id={"trade": hub}, device_id_type=MESH)

        gather(me - 1).start()
        settle(fact, pair_sem, 1)

        @pl.when(is_late)
        def _():
            each(lambda j: pair(j).start(), 0, near, among=False)

        def pass_on(j):
            @pl.when(jnp.logical_not(jnp.logical_and(me == slow, j >= n - 2)))
            def _():
                pair(j).start()

        each_odd(lambda j: pass_on(j - 1), base)
        each_odd(pass_on, base)

    for copy in copies:
        copy.wait()
    limit_copy.wait()
    tiled = (iota((F, LANES), 1) % F == iota((F, LANES), 0)).astype(f32).astype(bf16)
    diag = iota((LANES, DATES * K), 0) // F == iota((LANES, DATES * K), 1) // K
    rest = jnp.concatenate([load_v[...]] * DATES, axis=1)
    for i in range(3):
        piece = rest.astype(bf16)
        rest = rest - piece.astype(f32)
        wide = lax.dot_general(tiled, piece, (((0,), (0,)), ((), ())), preferred_element_type=f32)
        split[i * LANES : (i + 1) * LANES] = jnp.where(diag, wide, 0.0).astype(bf16)

    found = nrow_v[...] == iota((sets, sets), 0)
    owner_set = jnp.sum(jnp.where(found, iota((sets, sets), 1), 0).astype(f32), axis=1, keepdims=True)
    owner_set = owner_set.astype(jnp.int32)
    for c in range(slots // CHUNK):
        cut = slice(c * CHUNK, (c + 1) * CHUNK)
        onehot[:, cut] = (ids_v[:, cut] == owner_set).astype(f32).astype(bf16)

    for half in range(2):
        for i in range(LAG):
            held[half, :, i * paths : (i + 1) * paths] = marg_v[:, half * paths : (half + 1) * paths]

    live_now = live_count[0]
    slot_index = iota(size_v.shape, 0) * LANES + iota(size_v.shape, 1)
    used = jnp.where(slot_index < live_now, size_v[...], 0).astype(f32)
    basis_index = (iota((LANES, LANES), 1) % K).astype(f32)
    for c in range(slots // LANES):
        limit = jnp.broadcast_to(used[c : c + 1], (LANES, LANES)).T
        keep = basis_index < limit
        cut = slice(c * LANES, (c + 1) * LANES)
        for h in range(0, DATES * K, LANES):
            side = slice(h, h + LANES)
            coef_v[cut, side] = jnp.where(keep, coef_v[cut, side].astype(f32), 0.0).astype(bf16)

    def pass_coefs(j):
        return pltpu.make_async_remote_copy(
            src_ref=part_c.at[j],
            dst_ref=recv_c.at[me - pool],
            send_sem=cs_sem,
            recv_sem=cr_sem,
            device_id={"trade": j},
            device_id_type=MESH,
        )

    @pl.when(is_late)
    def _():
        total = None
        for c in range(slots // CHUNK):
            cut = slice(c * CHUNK, (c + 1) * CHUNK)
            term = jnp.dot(onehot[:, cut], coef_v[cut], preferred_element_type=f32)
            total = term if total is None else total + term
        for j in range(n):
            part_c[j] = total[j * owned : (j + 1) * owned]

        @pl.when(even)
        def _():
            settle(fact, gr_sem.at[3], 1)

        each(lambda j: pass_coefs(j).start(), 0, near, among=False)
        recv_c[me - pool] = part_c[me]

    def make_basis(half, hold=False):
        for j in range(near):

            def fill(j=j):
                block = fact[half * near + j].astype(f32)
                spread[j * rows : (j + 1) * rows] = block

            if hold and j < 2:
                pl.when(jnp.logical_not(is_final))(fill)

                @pl.when(is_final)
                def _():
                    spread[j * rows : (j + 1) * rows] = jnp.zeros((rows, spread.shape[1]), f32)

            else:
                fill()
        table = jnp.concatenate([spread[...].astype(bf16)] * 3, axis=1)
        bent = jnp.tanh(jnp.dot(table, split[...], preferred_element_type=f32))
        date = iota(bent.shape, 1) // K
        for d in range(DATES):
            basis[half, d * paths : (d + 1) * paths] = jnp.where(date == d, bent, 0.0).astype(bf16)

    def half_sums(half, hold=False):
        make_basis(half, hold)

        across = (((1,), (1,)), ((), ()))

        def block_sums(right):
            cuts = [slice(c * CHUNK, (c + 1) * CHUNK) for c in range(slots // CHUNK)]
            values = [
                lax.dot_general(coef_v[cut], right, across, preferred_element_type=f32).astype(bf16) for cut in cuts
            ]
            total = None
            for cut, value in zip(cuts, values):
                term = jnp.dot(onehot[:, cut], value, preferred_element_type=f32)
                total = term if total is None else total + term
            return total

        blocks = max(1, acc.shape[1] // COLS)
        if blocks == 1:
            acc[...] = block_sums(basis[half])
        else:

            def one(b, carry):
                side = pl.ds(pl.multiple_of(b * COLS, COLS), COLS)
                acc[:, side] = block_sums(basis[half, side])
                return carry

            lax.fori_loop(0, blocks, one, 0)
        for j in range(n):
            part[half, j] = acc[j * owned : (j + 1) * owned]

    def scatter(j, half, stage):
        return pltpu.make_async_remote_copy(
            src_ref=part.at[half, j],
            dst_ref=recv.at[half, me],
            send_sem=ss_sem.at[stage],
            recv_sem=sr_sem.at[half],
            device_id={"trade": j},
            device_id_type=MESH,
        )

    @pl.when(jnp.logical_and(is_early, even))
    def _():
        settle(fact, gr_sem.at[3], 1)

    @pl.when(is_final)
    def _():
        settle(fact, gr_sem.at[1], near - 4)

    @pl.when(jnp.logical_not(is_final))
    def _():
        settle(fact, gr_sem.at[mine], near - 2)

    def late_pair(j):
        held = pl.ds(near, 2)
        return pltpu.make_async_remote_copy(
            src_ref=fact.at[held],
            dst_ref=fact.at[held],
            send_sem=gs_sem,
            recv_sem=gr_sem.at[2],
            device_id={"trade": j},
            device_id_type=MESH,
        )

    @pl.when(me == helper)
    def _():
        late_pair(n - 2).start()
        late_pair(n - 1).start()

    @pl.when(is_hub)
    def _():
        pl.semaphore_wait(ready, 1)
        each(lambda i: relay(n - 1 - i).start(), 0, near, among=False)

    half_sums(mine, hold=True)

    @pl.when(is_late)
    def _():
        each(lambda j: scatter(j, mine, 0).start(), 0, n)
        each(lambda j: pass_coefs(j).start(), near, n)

    @pl.when(is_early)
    def _():
        each(lambda j: scatter(j, mine, 0).start(), 0, near)

    settle(fact, gr_sem.at[1 - mine], near)

    @pl.when(is_early)
    def _():
        each(lambda j: scatter(j, mine, 0).start(), near, n, among=False)


    @pl.when(is_early)
    def _():
        half_sums(1 - mine)
        each(lambda j: scatter(j, 1 - mine, 1).start(), 0, n)
        recv[1 - mine, me] = part[1 - mine, me]
        settle(recv_c, cr_sem, n - pool)

    @pl.when(is_late)
    def _():
        make_basis(1 - mine)

        @pl.when(is_final)
        def _():
            settle(fact, gr_sem.at[2], 2)
            make_basis(1)

        settle(recv_c, cr_sem, n - pool - 1)

    recv[mine, me] = part[mine, me]

    def pooled(first, half):
        rest = recv_c[first]
        for j in range(first + 1, n - pool):
            rest = rest + recv_c[j]
        pieces = []
        for i in range(3):
            pieces.append(rest.astype(bf16).astype(f32))
            rest = rest - pieces[i]
        stack = jnp.concatenate(pieces, axis=0).astype(bf16)
        thirds = lax.dot_general(stack, basis[half], (((1,), (1,)), ((), ())), preferred_element_type=f32)
        return thirds[2 * owned :] + thirds[owned : 2 * owned] + thirds[:owned]

    recv[0, pool] = pooled(0, 0)
    held_back = iota((owned, DATES * paths), 1) % paths < 2 * rows
    recv[1, me] = recv[1, me] + jnp.where(held_back, pooled(n - 2 - pool, 1), 0.0)
    for j in range(pool + 1, n):
        recv[0, j] = jnp.zeros(recv.shape[2:], f32)

    row_at = iota((owned, 1), 0)
    limits = jnp.zeros((owned, 1), f32)
    for r in range(owned):
        limits = jnp.where(row_at == r, thr_s[r], limits)
    first = LAG * paths
    result = jnp.zeros(out.shape, f32)
    lane_date = iota((owned, width), 1) // paths
    column = iota(out.shape, 1)

    def shortfall(half):
        netted = recv[half, 0]
        for j in range(1, n):
            netted = netted + recv[half, j]
        margin = jnp.maximum(netted[:, : (DATES - LAG) * paths] - limits, 0.0)
        collateral = jnp.concatenate([held[half], margin], axis=1)
        return jnp.maximum(netted - collateral, 0.0)

    @pl.when(is_early)
    def _():
        settle(recv.at[0], sr_sem.at[0], pool - 1)

    @pl.when(is_late)
    def _():
        settle(recv.at[0], sr_sem.at[0], pool)

    short = shortfall(0)
    settle(recv.at[1], sr_sem.at[1], n - 1)
    short = short + shortfall(1)
    for j in range(DATES // rep):
        block = short[:, j * width : (j + 1) * width]
        for i in range(rep):
            own_date = jnp.where(lane_date == i, block, 0.0) if rep > 1 else block
            result = jnp.where(column == j * rep + i, jnp.sum(own_date, axis=1, keepdims=True), result)
    out[...] = result

    @pl.when(jnp.logical_and(is_early, odd))
    def _():
        settle(fact, gs_sem, near)
        settle(fact, gs_sem, near - 3)

    @pl.when(is_hub)
    def _():
        each(lambda j: settle(fact, gs_sem, near), near, n, among=False)

    @pl.when(even)
    def _():
        settle(fact, gs_sem, 1)

    @pl.when(is_odd)
    def _():
        settle(fact, gs_sem, n)
        settle(fact, gs_sem, n - 7)

        @pl.when(me != slow)
        def _():
            settle(fact, gs_sem, 4)

        @pl.when(me == helper)
        def _():
            settle(fact, gs_sem, 4)

    settle(recv.at[0], ss_sem.at[0], n - 1)

    @pl.when(is_early)
    def _():
        settle(recv.at[1], ss_sem.at[1], n - 1)

    @pl.when(is_late)
    def _():
        settle(part_c, cs_sem, n - 1)


def stay(x):
    return pltpu.with_memory_space_constraint(x, pltpu.MemorySpace.HBM)


def body(n, factors, loadings, trade_coef, basis_size, set_ids, live_count, netting_row, threshold, margin_start):
    rows = factors.shape[0]
    paths = n * rows
    half = paths // 2
    rep = max(1, LANES // half)
    slots = trade_coef.shape[0]
    sets = netting_row.shape[0]
    owned = threshold.shape[0]
    wide = DATES * half
    hbm = pl.BlockSpec(memory_space=pltpu.MemorySpace.HBM)
    total = pl.pallas_call(
        functools.partial(kernel, n),
        out_shape=jax.ShapeDtypeStruct((owned, DATES), f32),
        in_specs=[hbm] * 5 + [pl.BlockSpec(memory_space=pltpu.SMEM)] + [hbm] * 3,
        out_specs=pl.BlockSpec(memory_space=pltpu.VMEM),
        scratch_shapes=[
            pltpu.VMEM((n, rows, DATES * F), bf16),
            pltpu.VMEM((F, K), f32),
            pltpu.VMEM((slots, DATES * K), bf16),
            pltpu.VMEM((slots // LANES, LANES), jnp.int32),
            pltpu.VMEM((1, slots), jnp.int32),
            pltpu.VMEM((1, sets), jnp.int32),
            pltpu.SMEM((owned,), f32),
            pltpu.VMEM((owned, paths), f32),
            pltpu.VMEM((3 * DATES * F, DATES * K), bf16),
            pltpu.VMEM((sets, slots), bf16),
            pltpu.VMEM((half, DATES * F), f32),
            pltpu.VMEM((2, wide, DATES * K), bf16),
            pltpu.VMEM((2, owned, LAG * half), f32),
            pltpu.VMEM((sets, wide), f32),
            pltpu.VMEM((2, n, owned, wide), f32),
            pltpu.VMEM((2, n, owned, wide), f32),
            pltpu.VMEM((n, owned, DATES * K), f32),
            pltpu.VMEM((n // 2, owned, DATES * K), f32),
            pltpu.SemaphoreType.DMA((3,)),
            pltpu.SemaphoreType.DMA,
            pltpu.SemaphoreType.DMA((4,)),
            pltpu.SemaphoreType.DMA,
            pltpu.SemaphoreType.DMA((2,)),
            pltpu.SemaphoreType.DMA((2,)),
            pltpu.SemaphoreType.DMA,
            pltpu.SemaphoreType.DMA,
            pltpu.SemaphoreType.REGULAR,
        ],
        compiler_params=pltpu.CompilerParams(
            collective_id=0, has_side_effects=True, vmem_limit_bytes=48 * 2**20
        ),
    )(
        stay(factors),
        stay(loadings.T),
        stay(trade_coef),
        stay(basis_size.reshape(slots // LANES, LANES)),
        stay(set_ids.reshape(1, slots)),
        live_count,
        stay(netting_row.reshape(1, sets)),
        stay(threshold),
        stay(margin_start),
    )
    return total / paths


def solution(mesh):
    return jax.shard_map(
        functools.partial(body, mesh.shape["trade"]),
        mesh=mesh,
        in_specs=(
            P(("group", "trade"), None),
            P(),
            P(("group", "trade"), None),
            P(("group", "trade")),
            P(("group", "trade")),
            P(("group", "trade")),
            P("group"),
            P(("group", "trade")),
            P(("group", "trade"), None),
        ),
        out_specs=P(("group", "trade"), None),
        check_vma=False,
    )
```
